32 devices in a mesh: grp: 2 (over x), wide: 16 (over z, y, core).
Axes of the slice: x: 2, y: 2, z: 4, core: 2. Of those that a mesh axis runs over, the one named last changes fastest.
Arguments:
- hidden: bfloat16 [32, 256, 8192], P(('grp', 'wide')), parts along dimension 0, may hold values from -6 to 6
- output_gradient: bfloat16 [32, 256, 8192], P(('grp', 'wide')), parts along dimension 0, may hold values from -6 to 6
- adapter_up_factor: bfloat16 [8192, 64], replicated, may hold values from -0.0625 to 0.0625
- first_moment_estimate: float32 [64, 8192], P(None, 'wide'), may hold values from -0.06 to 0.06
- second_moment_estimate: float32 [64, 8192], P(None, 'wide'), may hold values from 0.0001 to 0.01
- lengths: int32 [32], P(('grp', 'wide')), parts along dimension 0, may hold values from 32 to 256, as said below
- seeds: int32 [128], P('wide'), may hold values from 0 to 16777215
Outputs:
- features: float32 [32, 4096], P(('grp', 'wide')), parts along dimension 0
The draws below stay inside these ranges and needn't reach their ends.
There are 2 independent parts, one for each index of `grp`. The reference program is written for one: setup_inputs(seed, part) draws one part's arguments, and reference() takes and returns one part's arrays. A program takes and returns all parts, laid end to end along the dimension named above; an argument that names none is the same for every part. Nothing has to cross between parts.
Inputs may be any that keep to these rules, and one draw needn't show every extreme that they name: `lengths`: some sequence has exactly 256 live tokens and some has 32.
All inputs are finite; a program needn't handle non-finite values.
Results may differ from the reference program's by a relative error of at most 0.0039.
Values may be sent and summed in bfloat16 or wider, within the bound.
No kernel may reach another device: no remote copies, remote signals or barrier semaphores. Data moves between devices by JAX's collectives and lax.ppermute only.
A program may use at most 384 MiB of HBM per device.

```python
import math
import jax
import jax.numpy as jnp
from jax import lax

D = 8192
OUTPUT_FEATURES = 8192
ADAPTER_RANK = 64
K = 4096
CB = 64
RB = 8
LEN = 256
SEQS = 16


def draw_lengths(key, part):
    values = jax.random.randint(jax.random.fold_in(key, 11), (SEQS,), LEN // 8, LEN + 1)
    top_pos = jax.random.randint(jax.random.fold_in(key, 12), (), 0, SEQS)
    offset = jax.random.randint(jax.random.fold_in(key, 13), (), 1, SEQS)
    low_pos = (top_pos + offset) % SEQS
    values = values.at[top_pos].set(LEN)
    values = values.at[low_pos].set(LEN // 8)
    return values.astype(jnp.int32)


def set_ends(values, own_key, smallest, largest):
    extent = values.shape
    spot = [jax.random.randint(jax.random.fold_in(own_key, axis), (), 0, extent[axis]) for axis in range(len(extent))]
    values = values.at[tuple(spot)].set(smallest)
    longest = extent.index(max(extent))
    spot[longest] = (spot[longest] + 1) % extent[longest]
    return values.at[tuple(spot)].set(largest)


def block_scale(own_key, extent, split, low, largest):
    level = 1.0
    for dim, blocks in split:
        draws = jax.random.uniform(jax.random.fold_in(jax.random.fold_in(own_key, 6), dim), (blocks,), jnp.float32, low / len(split), largest / len(split))
        level = level * jnp.repeat(jnp.exp(draws), extent[dim] // blocks).reshape((-1,) + (1,) * (len(extent) - 1 - dim))
    return level


def normal_values(own_key, dims, width, most, shards=(), held_as=jnp.bfloat16):
    entries = jax.random.normal(own_key, dims, jnp.float32) * width
    if len(shards) > 0:
        entries = block_scale(own_key, dims, shards, -0.22, 0.18) * entries
    return jnp.clip(entries, min=-most, max=most).astype(held_as)


def setup_inputs(seed: int = 0, part: int = 0) -> dict:
    key_of = jax.random.split(jax.random.key(seed), 8)
    part_splits = jax.random.split(jax.random.fold_in(key_of[7], part), 8)
    hidden = normal_values(part_splits[0], (SEQS, LEN, D), 1.0, 6.0, ((0, 16),))
    output_gradient = normal_values(part_splits[1], (SEQS, LEN, OUTPUT_FEATURES), 1.0, 6.0, ((0, 16),))
    adapter_up_factor = normal_values(key_of[2], (OUTPUT_FEATURES, ADAPTER_RANK), OUTPUT_FEATURES ** -0.5, 0.0625)
    first_moment_estimate = normal_values(key_of[3], (ADAPTER_RANK, D), 0.01, 0.06, ((1, 16),), jnp.float32)
    second_moment_estimate = jnp.clip(jnp.exp(math.log(0.01) - 4.6051702 * jax.random.uniform(key_of[4], (ADAPTER_RANK, D), jnp.float32) ** block_scale(key_of[4], (ADAPTER_RANK, D), ((1, 16),), -0.2, 0.2)), 0.0001, 0.01)
    lengths = draw_lengths(jax.random.fold_in(jax.random.fold_in(key_of[7], part), 71), part)
    seeds = set_ends(jax.random.randint(key_of[6], (D // CB,), 0, 16777216), jax.random.fold_in(key_of[6], 1), 0, 16777215).astype(jnp.int32)
    return {"hidden": hidden, "output_gradient": output_gradient, "adapter_up_factor": adapter_up_factor, "first_moment_estimate": first_moment_estimate, "second_moment_estimate": second_moment_estimate, "lengths": lengths, "seeds": seeds}


def mix_bits(hashed):
    for turn in range(2):
        hashed = hashed & 2147483647
        hashed = hashed ^ jnp.right_shift(hashed, 16)
        hashed = hashed * 73244475
    hashed = hashed & 2147483647
    hashed = hashed ^ jnp.right_shift(hashed, 16)
    return hashed

def sign_block(tile_seed, first_param, param_count, feat_count):
    param_ids = first_param + lax.broadcasted_iota(jnp.int32, (param_count, feat_count), 0)
    feat_ids = lax.broadcasted_iota(jnp.int32, (param_count, feat_count), 1)
    hashed = mix_bits(param_ids * 1000003 + feat_ids * 7919 + tile_seed)
    return (1 - 2 * (hashed & 1)).astype(jnp.bfloat16)

def reference(hidden, output_gradient, adapter_up_factor, first_moment_estimate, second_moment_estimate, lengths, seeds):

    def seq_grad(inputs):
        tokens, gradient_results, live = inputs
        rank_reduced = jnp.dot(gradient_results, adapter_up_factor, preferred_element_type=jnp.float32)
        live_mask = jnp.arange(LEN, dtype=jnp.int32) < live
        rank_reduced = jnp.where(live_mask[:, None], rank_reduced, 0.0).astype(jnp.bfloat16)
        summed = jnp.dot(rank_reduced.T, tokens, preferred_element_type=jnp.float32)
        return (summed / live.astype(jnp.float32)).astype(jnp.bfloat16)
    seq_grads = lax.map(seq_grad, (hidden, output_gradient, lengths))
    grad_full = seq_grads.astype(jnp.float32)
    first_new = 0.9 * first_moment_estimate[None] + 0.1 * grad_full
    second_new = 0.999 * second_moment_estimate[None] + 0.001 * grad_full * grad_full
    update = (first_new / (jnp.sqrt(second_new) + 1e-08)).astype(jnp.bfloat16)
    row_groups = ADAPTER_RANK // RB
    steps_all = D // CB * row_groups

    def tile_step(loop_index, summed):
        loop_index = loop_index.astype(jnp.int32)
        col_pos = loop_index // row_groups
        grp_pos = loop_index % row_groups
        upd_block = lax.dynamic_slice(update, (jnp.int32(0), grp_pos * RB, col_pos * CB), (SEQS, RB, CB))
        upd_block = upd_block.reshape(SEQS, RB * CB)
        signs = sign_block(seeds[col_pos], grp_pos * (RB * CB), RB * CB, K)
        return summed + jnp.dot(upd_block, signs, preferred_element_type=jnp.float32)
    projected = lax.fori_loop(0, steps_all, tile_step, jnp.zeros((SEQS, K), jnp.float32))
    return projected * lax.rsqrt(lax.optimization_barrier(jnp.mean(projected * projected, axis=1, keepdims=True)) + 1e-06)
```

```python
import functools
import jax
import jax.numpy as jnp
from jax import lax
from jax.experimental import pallas as pl
from jax.experimental.pallas import tpu as pltpu
from jax.sharding import PartitionSpec as P

K = 4096
CB = 64
MUL = 73244475
TOP = (((MUL + 65536) << 15) + 2**31) % 2**32 - 2**31
LOW31 = 2147483647
ROW = 1000003
FEAT = 7919
AXES = ("grp", "wide")
LANES = 128
KT = 256


def shift_down(bits, places):
    return lax.shift_right_logical(bits, jnp.int32(places))


def sign_bits(hashed):
    hashed = (hashed ^ (shift_down(hashed, 16) & 32767)) * MUL
    hashed = (hashed ^ (shift_down(hashed, 16) & 32767)) * jnp.int32(TOP)
    return hashed < 0


def grad_kernel(lens_ref, up_ref, outg_ref, hid_ref, out_ref, acc_ref, low_ref, *, blocks, groups):
    seq, step = pl.program_id(0), pl.program_id(1)

    @pl.when(step == 0)
    def _():
        acc_ref[...] = jnp.zeros_like(acc_ref)

    @pl.when(step < blocks)
    def _():
        acc_ref[...] += lax.dot_general(
            up_ref[...], outg_ref[0], (((1,), (1,)), ((), ())), preferred_element_type=jnp.float32
        )

    @pl.when(step == blocks - 1)
    def _():
        live = lax.broadcasted_iota(jnp.int32, acc_ref.shape, 1) < lens_ref[seq]
        low_ref[...] = jnp.where(live, acc_ref[...], 0.0).astype(jnp.bfloat16)

    @pl.when(step >= blocks)
    def _():
        summed = jnp.dot(low_ref[...], hid_ref[0], preferred_element_type=jnp.float32)
        grad = (summed / lens_ref[seq].astype(jnp.float32)).astype(jnp.bfloat16)
        rows, cols = out_ref.shape[-2:]
        for grp in range(groups):
            for own in range(out_ref.shape[1]):
                out_ref[grp, own, 0] = grad[grp * rows : (grp + 1) * rows, own * cols : (own + 1) * cols]


def seq_grads(hidden, output_gradient, adapter_up_factor, lengths, groups, wide):
    seqs, toks, width = hidden.shape
    outs, rank = adapter_up_factor.shape
    rows, cols = rank // groups, width // wide
    blk = 1024
    blocks = width // blk
    return pl.pallas_call(
        functools.partial(grad_kernel, blocks=blocks, groups=groups),
        out_shape=jax.ShapeDtypeStruct((groups, wide, seqs, rows, cols), jnp.bfloat16),
        grid_spec=pltpu.PrefetchScalarGridSpec(
            num_scalar_prefetch=1,
            grid=(seqs, 2 * blocks),
            in_specs=[
                pl.BlockSpec((rank, outs // blocks), lambda s, i, n: (0, jnp.minimum(i, blocks - 1))),
                pl.BlockSpec((1, toks, outs // blocks), lambda s, i, n: (s, 0, jnp.minimum(i, blocks - 1))),
                pl.BlockSpec((1, toks, blk), lambda s, i, n: (s, 0, jnp.maximum(i - blocks, 0))),
            ],
            out_specs=pl.BlockSpec(
                (groups, blk // cols, 1, rows, cols), lambda s, i, n: (0, jnp.maximum(i - blocks, 0), s, 0, 0)
            ),
            scratch_shapes=[pltpu.VMEM((rank, toks), jnp.float32), pltpu.VMEM((rank, toks), jnp.bfloat16)],
        ),
        name="seq_grads",
    )(lengths, adapter_up_factor.T, output_gradient, hidden)


def project_kernel(
    seeds_ref, grp_ref, grad_ref, first_ref, second_ref, out_ref, wide_ref, upd_ref, sum_ref, pos_ref, *, per_loop
):
    step = pl.program_id(0)
    seqs, rows, cols = grad_ref.shape
    chunk = upd_ref.shape[2]
    halves = cols // chunk
    parts = chunk // CB

    @pl.when(step == 0)
    def _():
        pos_ref[...] = (
            lax.broadcasted_iota(jnp.int32, pos_ref.shape, 0) * ROW
            + lax.broadcasted_iota(jnp.int32, pos_ref.shape, 1) * FEAT
        )
        first_old = 0.9 * first_ref[...]
        second_old = 0.999 * second_ref[...]

        def update_step(seq, carry):
            grad = grad_ref[seq].astype(jnp.float32)
            first_new = first_old + 0.1 * grad
            second_new = second_old + 0.001 * grad * grad
            update = first_new / (jnp.sqrt(second_new) + 1e-08)
            for lane in range(0, cols, LANES):
                part = update[:, lane : lane + LANES]
                wide_ref[lane // LANES, pl.ds(pl.multiple_of(seq * rows, rows), rows), : part.shape[1]] = part
            return carry

        lax.fori_loop(0, seqs, update_step, 0)
        total = jnp.zeros((seqs, min(LANES, chunk)), jnp.float32)
        for row in range(rows):
            for half in range(halves):
                for lane in range(0, chunk, LANES):
                    upd = wide_ref[(half * chunk + lane) // LANES, pl.ds(row, seqs, stride=rows), :]
                    upd = upd[:, : min(LANES, chunk)].astype(jnp.bfloat16)
                    upd_ref[row * halves + half, :, lane : lane + upd.shape[1]] = upd
                    total += upd.astype(jnp.float32)
        sum_ref[...] = jnp.broadcast_to(jnp.sum(total, axis=1, keepdims=True), sum_ref.shape)

    base = grp_ref[0] * (rows * CB * ROW) + step * (KT * FEAT)

    def chunk_step(pos, acc):
        for sub in range(per_loop):
            entry = pos * per_loop + sub
            row, half = entry // halves, sub % halves
            origin = base + row * (CB * ROW)
            tile = [pos_ref[...] + (origin + seeds_ref[half * parts + part]) for part in range(parts)]
            bits = sign_bits(jnp.concatenate(tile, axis=0) if parts > 1 else tile[0])
            weights = jnp.where(bits, -2.0, 0.0).astype(jnp.bfloat16)
            acc += jnp.dot(upd_ref[entry], weights, preferred_element_type=jnp.float32)
        return acc

    start = jnp.broadcast_to(sum_ref[:, :1], (seqs, KT))
    acc = lax.fori_loop(0, upd_ref.shape[0] // per_loop, chunk_step, start)
    feats = out_ref.shape[0] // seqs
    for part in range(KT // LANES):
        out_ref[pl.ds(step * (KT // LANES) + part, seqs, stride=feats), :] = acc[:, part * LANES : (part + 1) * LANES]


def project(grads, first, second, seeds, grp):
    seqs, rows, cols = grads.shape
    chunk = min(256, cols)
    chunks = rows * cols // chunk
    feats = K // LANES
    return pl.pallas_call(
        functools.partial(project_kernel, per_loop=min(16, chunks)),
        out_shape=jax.ShapeDtypeStruct((seqs * feats, LANES), jnp.float32),
        grid_spec=pltpu.PrefetchScalarGridSpec(
            num_scalar_prefetch=2,
            grid=(K // KT,),
            in_specs=[
                pl.BlockSpec((seqs, rows, cols), lambda i, s, g: (0, 0, 0)),
                pl.BlockSpec((rows, cols), lambda i, s, g: (g[0], 0)),
                pl.BlockSpec((rows, cols), lambda i, s, g: (g[0], 0)),
            ],
            out_specs=pl.BlockSpec((seqs * feats, LANES), lambda i, s, g: (0, 0)),
            scratch_shapes=[
                pltpu.VMEM((pl.cdiv(cols, LANES), seqs * rows, LANES), jnp.float32),
                pltpu.VMEM((chunks, seqs, chunk), jnp.bfloat16),
                pltpu.VMEM((seqs, LANES), jnp.float32),
                pltpu.VMEM((CB, KT), jnp.int32),
            ],
        ),
        name="project",
    )(seeds, grp, grads, first, second)


def shards(
    hidden,
    output_gradient,
    adapter_up_factor,
    first_moment_estimate,
    second_moment_estimate,
    lengths,
    seeds,
):
    groups, wide = lax.axis_size("grp"), lax.axis_size("wide")
    devices = groups * wide
    own_seqs = hidden.shape[0]
    grads = seq_grads(hidden, output_gradient, adapter_up_factor, lengths, groups, wide)
    rows, cols = grads.shape[-2:]
    grads = grads.reshape(devices, own_seqs, rows, cols)
    grads = lax.all_to_all(grads, AXES, 0, 0, tiled=True).reshape(devices * own_seqs, rows, cols)
    grp = lax.axis_index("grp").astype(jnp.int32).reshape(1)
    partial = project(grads, first_moment_estimate, second_moment_estimate, seeds, grp)
    partial = partial.reshape(devices, own_seqs, K // LANES, LANES)
    partial = lax.all_to_all(partial, AXES, 0, 0, tiled=True)
    own_rows = jnp.sum(partial, axis=0)
    scale = lax.rsqrt(jnp.mean(own_rows * own_rows, axis=(1, 2), keepdims=True) + 1e-06)
    return (own_rows * scale).reshape(own_seqs, K)


def solution(mesh):
    placed = (
        P(AXES, None, None),
        P(AXES, None, None),
        P(),
        P(None, "wide"),
        P(None, "wide"),
        P(AXES),
        P("wide"),
    )
    with jax.sharding.use_abstract_mesh(mesh.abstract_mesh):
        return jax.shard_map(shards, mesh=mesh, in_specs=placed, out_specs=P(AXES, None), check_vma=False)
```

```python
import functools
import jax
import jax.numpy as jnp
from jax import lax
from jax.experimental import pallas as pl
from jax.experimental.pallas import tpu as pltpu
from jax.sharding import PartitionSpec as P

K = 4096
CB = 64
MUL = 73244475
TOP = (((MUL + 65536) << 15) + 2**31) % 2**32 - 2**31
LOW31 = 2147483647
ROW = 1000003
FEAT = 7919
AXES = ("grp", "wide")
LANES = 128
KT = 256
STRIDE = 3


def shift_down(bits, places):
    return lax.shift_right_logical(bits, jnp.int32(places))


def sign_bits(hashed):
    hashed = (hashed ^ (shift_down(hashed, 16) & 32767)) * MUL
    hashed = (hashed ^ (shift_down(hashed, 16) & 32767)) * jnp.int32(TOP)
    return hashed < 0


def grad_kernel(lens_ref, up_ref, outg_ref, hid_ref, out_ref, acc_ref, low_ref, *, blocks, groups):
    seq, step = pl.program_id(0), pl.program_id(1)

    @pl.when(step == 0)
    def _():
        acc_ref[...] = jnp.zeros_like(acc_ref)

    @pl.when(step < blocks)
    def _():
        acc_ref[...] += lax.dot_general(
            up_ref[...], outg_ref[0], (((1,), (1,)), ((), ())), preferred_element_type=jnp.float32
        )

    @pl.when(step == blocks - 1)
    def _():
        live = lax.broadcasted_iota(jnp.int32, acc_ref.shape, 1) < lens_ref[seq]
        low_ref[...] = jnp.where(live, acc_ref[...], 0.0).astype(jnp.bfloat16)

    @pl.when(step >= blocks)
    def _():
        summed = jnp.dot(low_ref[...], hid_ref[0], preferred_element_type=jnp.float32)
        grad = (summed / lens_ref[seq].astype(jnp.float32)).astype(jnp.bfloat16)
        rows, cols = out_ref.shape[-2:]
        for grp in range(groups):
            for own in range(out_ref.shape[1]):
                out_ref[grp, own, 0] = grad[grp * rows : (grp + 1) * rows, own * cols : (own + 1) * cols]


def seq_grads(hidden, output_gradient, adapter_up_factor, lengths, groups, wide):
    seqs, toks, width = hidden.shape
    outs, rank = adapter_up_factor.shape
    rows, cols = rank // groups, width // wide
    blk = 1024
    blocks = width // blk
    return pl.pallas_call(
        functools.partial(grad_kernel, blocks=blocks, groups=groups),
        out_shape=jax.ShapeDtypeStruct((groups, wide, seqs, rows, cols), jnp.bfloat16),
        grid_spec=pltpu.PrefetchScalarGridSpec(
            num_scalar_prefetch=1,
            grid=(seqs, 2 * blocks),
            in_specs=[
                pl.BlockSpec((rank, outs // blocks), lambda s, i, n: (0, jnp.minimum(i, blocks - 1))),
                pl.BlockSpec((1, toks, outs // blocks), lambda s, i, n: (s, 0, jnp.minimum(i, blocks - 1))),
                pl.BlockSpec((1, toks, blk), lambda s, i, n: (s, 0, jnp.maximum(i - blocks, 0))),
            ],
            out_specs=pl.BlockSpec(
                (groups, blk // cols, 1, rows, cols), lambda s, i, n: (0, jnp.maximum(i - blocks, 0), s, 0, 0)
            ),
            scratch_shapes=[pltpu.VMEM((rank, toks), jnp.float32), pltpu.VMEM((rank, toks), jnp.bfloat16)],
        ),
        name="seq_grads",
    )(lengths, adapter_up_factor.T, output_gradient, hidden)


def fill_positions(pos_ref):
    pos_ref[...] = (
        lax.broadcasted_iota(jnp.int32, pos_ref.shape, 0) * ROW
        + lax.broadcasted_iota(jnp.int32, pos_ref.shape, 1) * FEAT
    )


def sign_weights(pos_ref, seeds_ref, origin, half, parts):
    tile = [pos_ref[...] + (origin + seeds_ref[half * parts + part]) for part in range(parts)]
    bits = sign_bits(jnp.concatenate(tile, axis=0) if parts > 1 else tile[0])
    return jnp.where(bits, -2.0, 0.0).astype(jnp.bfloat16)


def presign_kernel(seeds_ref, grp_ref, out_ref, pos_ref, *, rows, halves):
    tile, block = pl.program_id(0), pl.program_id(1)

    @pl.when((tile == 0) & (block == 0))
    def _():
        fill_positions(pos_ref)

    base = grp_ref[0] * (rows * CB * ROW) + tile * (KT * FEAT)
    per_block, chunk = out_ref.shape[1:3]
    for sub in range(per_block):
        row, half = (block * per_block + sub) // halves, sub % halves
        out_ref[0, sub] = sign_weights(pos_ref, seeds_ref, base + row * (CB * ROW), half, chunk // CB)


def presign(seeds, grp, rows, cols):
    chunk = min(256, cols)
    chunks = rows * cols // chunk
    per_block = min(16, chunks)
    tiles = K // KT // STRIDE
    return pl.pallas_call(
        functools.partial(presign_kernel, rows=rows, halves=cols // chunk),
        out_shape=jax.ShapeDtypeStruct((tiles, chunks, chunk, KT), jnp.bfloat16),
        grid_spec=pltpu.PrefetchScalarGridSpec(
            num_scalar_prefetch=2,
            grid=(tiles, chunks // per_block),
            out_specs=pl.BlockSpec((1, per_block, chunk, KT), lambda i, j, s, g: (i, j, 0, 0)),
            scratch_shapes=[pltpu.VMEM((CB, KT), jnp.int32)],
        ),
        cost_estimate=pl.CostEstimate(
            flops=tiles * rows * cols * KT * 10, bytes_accessed=tiles * rows * cols * KT * 2, transcendentals=0
        ),
        name="presign",
    )(seeds, grp)


def project_kernel(
    seeds_ref,
    grp_ref,
    grad_ref,
    first_ref,
    second_ref,
    held_ref,
    out_ref,
    wide_ref,
    upd_ref,
    sum_ref,
    pos_ref,
    *,
    per_loop,
):
    step = pl.program_id(0)
    held = step % STRIDE == STRIDE - 1
    held_tiles = pl.num_programs(0) // STRIDE
    seqs, rows, cols = grad_ref.shape
    chunk = upd_ref.shape[2]
    halves = cols // chunk
    parts = chunk // CB

    @pl.when(step == 0)
    def _():
        fill_positions(pos_ref)
        first_old = 0.9 * first_ref[...]
        second_old = 0.999 * second_ref[...]

        def update_step(seq, carry):
            grad = grad_ref[seq].astype(jnp.float32)
            first_new = first_old + 0.1 * grad
            second_new = second_old + 0.001 * grad * grad
            update = first_new / (jnp.sqrt(second_new) + 1e-08)
            for lane in range(0, cols, LANES):
                part = update[:, lane : lane + LANES]
                wide_ref[lane // LANES, pl.ds(pl.multiple_of(seq * rows, rows), rows), : part.shape[1]] = part
            return carry

        lax.fori_loop(0, seqs, update_step, 0)
        total = jnp.zeros((seqs, min(LANES, chunk)), jnp.float32)
        for row in range(rows):
            for half in range(halves):
                for lane in range(0, chunk, LANES):
                    upd = wide_ref[(half * chunk + lane) // LANES, pl.ds(row, seqs, stride=rows), :]
                    upd = upd[:, : min(LANES, chunk)].astype(jnp.bfloat16)
                    upd_ref[row * halves + half, :, lane : lane + upd.shape[1]] = upd
                    total += upd.astype(jnp.float32)
        sum_ref[...] = jnp.broadcast_to(jnp.sum(total, axis=1, keepdims=True), sum_ref.shape)

    feats = out_ref.shape[0] // seqs
    start = jnp.broadcast_to(sum_ref[:, :1], (seqs, KT))

    def put(tile, acc):
        for part in range(KT // LANES):
            spot = tile * (KT // LANES) + part
            out_ref[pl.ds(spot, seqs, stride=feats), :] = acc[:, part * LANES : (part + 1) * LANES]

    @pl.when(held)
    def _():
        def chunk_step(pos, acc):
            for sub in range(per_loop):
                entry = pos * per_loop + sub
                acc += jnp.dot(upd_ref[entry], held_ref[0, entry], preferred_element_type=jnp.float32)
            return acc

        put(step // STRIDE, lax.fori_loop(0, upd_ref.shape[0] // per_loop, chunk_step, start))

    @pl.when(jnp.logical_not(held))
    def _():
        tile = held_tiles + step - step // STRIDE
        base = grp_ref[0] * (rows * CB * ROW) + tile * (KT * FEAT)

        def chunk_step(pos, acc):
            for sub in range(per_loop):
                entry = pos * per_loop + sub
                row, half = entry // halves, sub % halves
                weights = sign_weights(pos_ref, seeds_ref, base + row * (CB * ROW), half, parts)
                acc += jnp.dot(upd_ref[entry], weights, preferred_element_type=jnp.float32)
            return acc

        put(tile, lax.fori_loop(0, upd_ref.shape[0] // per_loop, chunk_step, start))


def project(grads, first, second, seeds, grp, held):
    seqs, rows, cols = grads.shape
    chunk = min(256, cols)
    chunks = rows * cols // chunk
    feats = K // LANES
    return pl.pallas_call(
        functools.partial(project_kernel, per_loop=min(16, chunks)),
        out_shape=jax.ShapeDtypeStruct((seqs * feats, LANES), jnp.float32),
        grid_spec=pltpu.PrefetchScalarGridSpec(
            num_scalar_prefetch=2,
            grid=(K // KT,),
            in_specs=[
                pl.BlockSpec(memory_space=pltpu.VMEM),
                pl.BlockSpec((rows, cols), lambda i, s, g: (g[0], 0)),
                pl.BlockSpec((rows, cols), lambda i, s, g: (g[0], 0)),
                pl.BlockSpec(
                    (1, chunks, chunk, KT), lambda i, s, g: (jnp.maximum(i - STRIDE + 2, 0) // STRIDE, 0, 0, 0)
                ),
            ],
            out_specs=pl.BlockSpec((seqs * feats, LANES), lambda i, s, g: (0, 0)),
            scratch_shapes=[
                pltpu.VMEM((pl.cdiv(cols, LANES), seqs * rows, LANES), jnp.float32),
                pltpu.VMEM((chunks, seqs, chunk), jnp.bfloat16),
                pltpu.VMEM((seqs, LANES), jnp.float32),
                pltpu.VMEM((CB, KT), jnp.int32),
            ],
        ),
        name="project",
    )(seeds, grp, grads, first, second, held)


def shards(
    hidden,
    output_gradient,
    adapter_up_factor,
    first_moment_estimate,
    second_moment_estimate,
    lengths,
    seeds,
):
    groups, wide = lax.axis_size("grp"), lax.axis_size("wide")
    devices = groups * wide
    own_seqs = hidden.shape[0]
    grads = seq_grads(hidden, output_gradient, adapter_up_factor, lengths, groups, wide)
    rows, cols = grads.shape[-2:]
    grp = lax.axis_index("grp").astype(jnp.int32).reshape(1)
    grads = grads.reshape(devices, own_seqs, rows, cols)
    held = presign(seeds, grp, rows, cols)
    grads = lax.all_to_all(grads, AXES, 0, 0, tiled=True).reshape(devices * own_seqs, rows, cols)
    partial = project(grads, first_moment_estimate, second_moment_estimate, seeds, grp, held)
    partial = partial.reshape(devices, own_seqs, K // LANES, LANES)
    partial = lax.all_to_all(partial, AXES, 0, 0, tiled=True)
    own_rows = jnp.sum(partial, axis=0)
    scale = lax.rsqrt(jnp.mean(own_rows * own_rows, axis=(1, 2), keepdims=True) + 1e-06)
    return (own_rows * scale).reshape(own_seqs, K)


def solution(mesh):
    placed = (
        P(AXES, None, None),
        P(AXES, None, None),
        P(),
        P(None, "wide"),
        P(None, "wide"),
        P(AXES),
        P("wide"),
    )
    with jax.sharding.use_abstract_mesh(mesh.abstract_mesh):
        return jax.shard_map(shards, mesh=mesh, in_specs=placed, out_specs=P(AXES, None), check_vma=False)
```

```python
import functools
import jax
import jax.numpy as jnp
from jax import lax
from jax.experimental import pallas as pl
from jax.experimental.pallas import tpu as pltpu
from jax.sharding import PartitionSpec as P

K = 4096
CB = 64
MUL = 73244475
TOP = (((MUL + 65536) << 15) + 2**31) % 2**32 - 2**31
LOW31 = 2147483647
ROW = 1000003
FEAT = 7919
AXES = ("grp", "wide")
LANES = 128
KT = 256
SLAB = 128
SLABS = 10
SEQ_BLOCK = 16


def shift_down(bits, places):
    return lax.shift_right_logical(bits, jnp.int32(places))


def mixed(hashed, wraps):
    top = shift_down(hashed, 16)
    if wraps:
        top = top & 32767
    hashed = (hashed ^ top) * MUL
    return (hashed ^ (shift_down(hashed, 16) & 32767)) * jnp.int32(TOP)


def sign_weights(top):
    return jnp.where(top < 0, -2.0, 0.0).astype(jnp.bfloat16)


def grad_kernel(lens_ref, up_any, outg_any, hid_any, out_ref, up_ref, outg_ref, hid_ref, sems):
    seq = pl.program_id(0)
    blocks, toks, outs = outg_ref.shape
    width = hid_ref.shape[2]
    groups, wide, _, rows, cols = out_ref.shape

    def loads(blk):
        return (
            pltpu.make_async_copy(up_any.at[:, pl.ds(blk * outs, outs)], up_ref.at[blk], sems.at[0, blk]),
            pltpu.make_async_copy(outg_any.at[seq, :, pl.ds(blk * outs, outs)], outg_ref.at[blk], sems.at[1, blk]),
            pltpu.make_async_copy(hid_any.at[seq, :, pl.ds(blk * width, width)], hid_ref.at[blk], sems.at[2, blk]),
        )

    copies = [loads(blk) for blk in range(blocks)]
    for load_up, load_outg, _ in copies:
        load_up.start()
        load_outg.start()
    for _, _, load_hid in copies:
        load_hid.start()
    low = jnp.zeros((toks, up_ref.shape[1]), jnp.float32)
    for blk, (load_up, load_outg, _) in enumerate(copies):
        load_up.wait()
        load_outg.wait()
        low += lax.dot_general(
            outg_ref[blk], up_ref[blk], (((1,), (1,)), ((), ())), preferred_element_type=jnp.float32
        )
    live = lax.broadcasted_iota(jnp.int32, low.shape, 0) < lens_ref[seq]
    low = jnp.where(live, low, 0.0).T.astype(jnp.bfloat16)
    count = lens_ref[seq].astype(jnp.float32)
    for blk, (_, _, load_hid) in enumerate(copies):
        load_hid.wait()
        summed = jnp.dot(low, hid_ref[blk], preferred_element_type=jnp.float32)
        grad = (summed / count).astype(jnp.bfloat16)
        for grp in range(groups):
            for own in range(width // cols):
                out_ref[grp, blk * (width // cols) + own, 0] = grad[
                    grp * rows : (grp + 1) * rows, own * cols : (own + 1) * cols
                ]


def seq_grads(hidden, output_gradient, adapter_up_factor, lengths, groups, wide):
    seqs, toks, width = hidden.shape
    outs, rank = adapter_up_factor.shape
    rows, cols = rank // groups, width // wide
    blocks = 4
    return pl.pallas_call(
        grad_kernel,
        out_shape=jax.ShapeDtypeStruct((groups, wide, seqs, rows, cols), jnp.bfloat16),
        grid_spec=pltpu.PrefetchScalarGridSpec(
            num_scalar_prefetch=1,
            grid=(seqs,),
            in_specs=[pl.BlockSpec(memory_space=pl.ANY)] * 3,
            out_specs=pl.BlockSpec((groups, wide, 1, rows, cols), lambda s, n: (0, 0, s, 0, 0)),
            scratch_shapes=[
                pltpu.VMEM((blocks, rank, outs // blocks), jnp.bfloat16),
                pltpu.VMEM((blocks, toks, outs // blocks), jnp.bfloat16),
                pltpu.VMEM((blocks, toks, width // blocks), jnp.bfloat16),
                pltpu.SemaphoreType.DMA((3, blocks)),
            ],
        ),
        name="seq_grads",
    )(lengths, adapter_up_factor.T, output_gradient, hidden)


def fill_positions(pos_ref):
    pos_ref[...] = (
        lax.broadcasted_iota(jnp.int32, pos_ref.shape, 0) * ROW
        + lax.broadcasted_iota(jnp.int32, pos_ref.shape, 1) * FEAT
    )


BLOCK = CB * ROW
SPAN = (CB - 1) * ROW + (K - 1) * FEAT
EDGE = 2**31 - SPAN


def fill_turns(turn_ref, seeds_ref, first_row, rows):
    for pos in range(turn_ref.shape[0]):
        short = EDGE - ((seeds_ref[pos] + first_row * BLOCK) & LOW31)
        turn_ref[pos] = lax.div(jnp.maximum(short + (BLOCK - 1), 0), jnp.int32(BLOCK)) + 2


def slot_row(turn, slot, rows):
    return lax.rem(turn + slot, jnp.int32(rows))


def slot_wraps(slot, rows):
    return slot >= rows - 2 or rows * BLOCK + SPAN > 2**31


def slot_tile(pos_ref, seeds_ref, turn_ref, first_row, feat, slot, half, parts, rows):
    tile = []
    for part in range(half * parts, (half + 1) * parts):
        row = first_row + slot_row(turn_ref[part], slot, rows)
        tile.append(pos_ref[...] + ((seeds_ref[part] + row * BLOCK + feat * FEAT) & LOW31))
    return mixed(jnp.concatenate(tile, axis=0) if parts > 1 else tile[0], slot_wraps(slot, rows))


def presign_kernel(seeds_ref, grp_ref, out_ref, pos_ref, turn_ref, *, rows, halves):
    slab = pl.program_id(0)
    first_row = grp_ref[0] * rows
    pairs, chunk, feats = out_ref.shape[1:]

    @pl.when(slab == 0)
    def _():
        fill_positions(pos_ref)
        fill_turns(turn_ref, seeds_ref, first_row, rows)

    def top_of(entry):
        slot, half = divmod(entry, halves)
        return slot_tile(pos_ref, seeds_ref, turn_ref, first_row, slab * feats, slot, half, chunk // CB, rows)

    for pair in range(pairs):
        out_ref[0, pair] = top_of(2 * pair) | shift_down(top_of(2 * pair + 1), 17)


def presign(seeds, grp, rows, cols):
    chunk = min(256, cols)
    chunks = rows * cols // chunk
    return pl.pallas_call(
        functools.partial(presign_kernel, rows=rows, halves=cols // chunk),
        out_shape=jax.ShapeDtypeStruct((SLABS, chunks // 2, chunk, SLAB), jnp.int32),
        grid_spec=pltpu.PrefetchScalarGridSpec(
            num_scalar_prefetch=2,
            grid=(SLABS,),
            out_specs=pl.BlockSpec((1, chunks // 2, chunk, SLAB), lambda i, s, g: (i, 0, 0, 0)),
            scratch_shapes=[pltpu.VMEM((CB, SLAB), jnp.int32), pltpu.SMEM((cols // CB,), jnp.int32)],
        ),
        cost_estimate=pl.CostEstimate(
            flops=SLABS * SLAB * rows * cols * 10, bytes_accessed=SLABS * SLAB * rows * cols * 2, transcendentals=0
        ),
        name="presign",
    )(seeds, grp)


def project_kernel(
    seeds_ref,
    grp_ref,
    grad_ref,
    first_ref,
    second_ref,
    held_ref,
    out_ref,
    wide_ref,
    upd_ref,
    sum_ref,
    pos_ref,
    turn_ref,
):
    step = pl.program_id(0)
    seqs, rows, cols = grad_ref.shape
    chunk = upd_ref.shape[2]
    halves = cols // chunk
    parts = chunk // CB
    first_row = grp_ref[0] * rows

    @pl.when(step == 0)
    def _():
        fill_positions(pos_ref)
        fill_turns(turn_ref, seeds_ref, first_row, rows)
        width = min(LANES, cols)

        def update_step(blk, carry):
            at = pl.ds(pl.multiple_of(blk * SEQ_BLOCK, SEQ_BLOCK), SEQ_BLOCK)
            for row in range(0, rows, 8):
                for lane in range(0, cols, LANES):
                    spot = (slice(row, row + 8), slice(lane, lane + width))
                    grad = grad_ref[(at, *spot)].astype(jnp.float32)
                    first_new = 0.9 * first_ref[spot] + 0.1 * grad
                    second_new = 0.999 * second_ref[spot] + 0.001 * grad * grad
                    update = first_new / (jnp.sqrt(second_new) + 1e-08)
                    update = jnp.swapaxes(update, 0, 1).astype(jnp.bfloat16)
                    wide_ref[lane // LANES, row : row + 8, at, :width] = update
            return carry

        lax.fori_loop(0, seqs // SEQ_BLOCK, update_step, 0)
        total = jnp.zeros((seqs, width), jnp.float32)
        lanes = lax.broadcasted_iota(jnp.int32, (seqs, LANES), 1)
        for entry in range(upd_ref.shape[0]):
            slot, half = divmod(entry, halves)
            for lane in range(0, chunk, LANES):
                spot = half * chunk + lane
                upd = wide_ref[spot // LANES, slot_row(turn_ref[spot // CB], slot, rows)]
                for pos in range(CB, width, CB):
                    row = slot_row(turn_ref[(spot + pos) // CB], slot, rows)
                    upd = jnp.where(lanes < pos, upd, wide_ref[spot // LANES, row])
                upd = upd[:, :width]
                upd_ref[entry, :, lane : lane + width] = upd
                total += upd.astype(jnp.float32)
        sum_ref[...] = jnp.broadcast_to(jnp.sum(total, axis=1, keepdims=True), sum_ref.shape)

    feats = out_ref.shape[0] // seqs
    held_feats = SLABS * SLAB
    start = jnp.broadcast_to(sum_ref[:, :1], (seqs, KT))

    def put(first_feat, acc):
        for part in range(acc.shape[1] // LANES):
            out_ref[pl.ds(first_feat // LANES + part, seqs, stride=feats), :] = acc[:, part * LANES : (part + 1) * LANES]

    def tile_step(with_held):
        feat = held_feats + step * KT
        acc, held_acc = start, start[:, :SLAB]
        for entry in range(upd_ref.shape[0]):
            slot, half = divmod(entry, halves)
            weights = sign_weights(slot_tile(pos_ref, seeds_ref, turn_ref, first_row, feat, slot, half, parts, rows))
            acc += jnp.dot(upd_ref[entry], weights, preferred_element_type=jnp.float32)
            if with_held:
                top = held_ref[0, entry // 2]
                weights = sign_weights(top << 17 if entry % 2 else top)
                held_acc += jnp.dot(upd_ref[entry], weights, preferred_element_type=jnp.float32)
        put(feat, acc)
        if with_held:
            put(step * SLAB, held_acc)

    pl.when(step < SLABS)(lambda: tile_step(True))
    pl.when(step >= SLABS)(lambda: tile_step(False))


def project(grads, first, second, seeds, grp, held):
    seqs, rows, cols = grads.shape
    chunk = min(256, cols)
    chunks = rows * cols // chunk
    feats = K // LANES
    return pl.pallas_call(
        project_kernel,
        out_shape=jax.ShapeDtypeStruct((seqs * feats, LANES), jnp.float32),
        grid_spec=pltpu.PrefetchScalarGridSpec(
            num_scalar_prefetch=2,
            grid=((K - SLABS * SLAB) // KT,),
            in_specs=[
                pl.BlockSpec(memory_space=pltpu.VMEM),
                pl.BlockSpec((rows, cols), lambda i, s, g: (g[0], 0)),
                pl.BlockSpec((rows, cols), lambda i, s, g: (g[0], 0)),
                pl.BlockSpec((1, chunks // 2, chunk, SLAB), lambda i, s, g: (jnp.minimum(i, SLABS - 1), 0, 0, 0)),
            ],
            out_specs=pl.BlockSpec((seqs * feats, LANES), lambda i, s, g: (0, 0)),
            scratch_shapes=[
                pltpu.VMEM((pl.cdiv(cols, LANES), rows, seqs, LANES), jnp.bfloat16),
                pltpu.VMEM((chunks, seqs, chunk), jnp.bfloat16),
                pltpu.VMEM((seqs, LANES), jnp.float32),
                pltpu.VMEM((CB, KT), jnp.int32),
                pltpu.SMEM((cols // CB,), jnp.int32),
            ],
        ),
        name="project",
    )(seeds, grp, grads, first, second, held)


def shards(
    hidden,
    output_gradient,
    adapter_up_factor,
    first_moment_estimate,
    second_moment_estimate,
    lengths,
    seeds,
):
    groups, wide = lax.axis_size("grp"), lax.axis_size("wide")
    devices = groups * wide
    own_seqs = hidden.shape[0]
    grads = seq_grads(hidden, output_gradient, adapter_up_factor, lengths, groups, wide)
    rows, cols = grads.shape[-2:]
    grp = lax.axis_index("grp").astype(jnp.int32).reshape(1)
    grads = grads.reshape(devices, own_seqs, rows, cols)
    held = presign(seeds, grp, rows, cols)
    grads = lax.all_to_all(grads, AXES, 0, 0, tiled=True).reshape(devices * own_seqs, rows, cols)
    partial = project(grads, first_moment_estimate, second_moment_estimate, seeds, grp, held)
    partial = partial.reshape(devices, own_seqs, K // LANES, LANES)
    partial = lax.all_to_all(partial, AXES, 0, 0, tiled=True)
    own_rows = jnp.sum(partial, axis=0)
    scale = lax.rsqrt(jnp.mean(own_rows * own_rows, axis=(1, 2), keepdims=True) + 1e-06)
    return (own_rows * scale).reshape(own_seqs, K)


def solution(mesh):
    placed = (
        P(AXES, None, None),
        P(AXES, None, None),
        P(),
        P(None, "wide"),
        P(None, "wide"),
        P(AXES),
        P("wide"),
    )
    with jax.sharding.use_abstract_mesh(mesh.abstract_mesh):
        return jax.shard_map(shards, mesh=mesh, in_specs=placed, out_specs=P(AXES, None), check_vma=False)
```

```python
import functools
import jax
import jax.numpy as jnp
from jax import lax
from jax.experimental import pallas as pl
from jax.experimental.pallas import tpu as pltpu
from jax.sharding import PartitionSpec as P

K = 4096
CB = 64
MUL = 73244475
TOP = (((MUL + 65536) << 15) + 2**31) % 2**32 - 2**31
LOW31 = 2147483647
ROW = 1000003
FEAT = 7919
AXES = ("grp", "wide")
LANES = 128
KT = 256
SLAB = 128
SLABS = 12
EARLY = 2
SEQ_BLOCK = 16
PROJECT_VMEM = 36 << 20


def shift_down(bits, places):
    return lax.shift_right_logical(bits, jnp.int32(places))


def mixed(hashed, wraps):
    top = shift_down(hashed, 16)
    if wraps:
        top = top & 32767
    hashed = (hashed ^ top) * MUL
    return (hashed ^ (shift_down(hashed, 16) & 32767)) * jnp.int32(TOP)


def sign_weights(top):
    return jnp.where(top < 0, -2.0, 0.0).astype(jnp.bfloat16)


def grad_kernel(
    lens_ref,
    seeds_ref,
    grp_ref,
    up_any,
    outg_any,
    hid_any,
    out_ref,
    held_any,
    up_ref,
    outg_ref,
    hid_ref,
    pos_ref,
    turn_ref,
    held_ref,
    sems,
    held_sems,
):
    seq = pl.program_id(0)
    blocks, toks, outs = outg_ref.shape
    width = hid_ref.shape[2]
    groups, wide, _, rows, cols = out_ref.shape
    chunk = held_ref.shape[2]
    first_row = grp_ref[0] * rows

    def loads(blk):
        return (
            pltpu.make_async_copy(up_any.at[:, pl.ds(blk * outs, outs)], up_ref.at[blk], sems.at[0, blk]),
            pltpu.make_async_copy(outg_any.at[seq, :, pl.ds(blk * outs, outs)], outg_ref.at[blk], sems.at[1, blk]),
            pltpu.make_async_copy(hid_any.at[seq, :, pl.ds(blk * width, width)], hid_ref.at[blk], sems.at[2, blk]),
        )

    copies = [loads(blk) for blk in range(blocks)]
    for load_up, load_outg, _ in copies:
        load_up.start()
        load_outg.start()
    for _, _, load_hid in copies:
        load_hid.start()

    def hold(slab):
        @pl.when(seq == 0)
        def _():
            for pair, word in slab_pairs(pos_ref, seeds_ref, turn_ref, first_row, slab, rows, cols // chunk, chunk):
                held_ref[slab, pair] = word
            pltpu.make_async_copy(held_ref.at[slab], held_any.at[slab], held_sems.at[slab]).start()

    @pl.when(seq == 0)
    def _():
        fill_positions(pos_ref)
        fill_turns(turn_ref, seeds_ref, first_row, rows)

    hold(0)
    low = jnp.zeros((toks, up_ref.shape[1]), jnp.float32)
    for blk, (load_up, load_outg, _) in enumerate(copies):
        load_up.wait()
        load_outg.wait()
        low += lax.dot_general(
            outg_ref[blk], up_ref[blk], (((1,), (1,)), ((), ())), preferred_element_type=jnp.float32
        )
    live = lax.broadcasted_iota(jnp.int32, low.shape, 0) < lens_ref[seq]
    low = jnp.where(live, low, 0.0).T.astype(jnp.bfloat16)
    count = lens_ref[seq].astype(jnp.float32)
    hold(1)
    for blk, (_, _, load_hid) in enumerate(copies):
        load_hid.wait()
        summed = jnp.dot(low, hid_ref[blk], preferred_element_type=jnp.float32)
        grad = (summed / count).astype(jnp.bfloat16)
        for grp in range(groups):
            for own in range(width // cols):
                out_ref[grp, blk * (width // cols) + own, 0] = grad[
                    grp * rows : (grp + 1) * rows, own * cols : (own + 1) * cols
                ]

    @pl.when(seq == 0)
    def _():
        for slab in range(EARLY):
            pltpu.make_async_copy(held_ref.at[slab], held_any.at[slab], held_sems.at[slab]).wait()


def seq_grads(hidden, output_gradient, adapter_up_factor, lengths, seeds, grp, groups, wide):
    seqs, toks, width = hidden.shape
    outs, rank = adapter_up_factor.shape
    rows, cols = rank // groups, width // wide
    chunk = min(256, cols)
    pairs = rows * cols // chunk // 2
    blocks = 4
    return pl.pallas_call(
        grad_kernel,
        out_shape=(
            jax.ShapeDtypeStruct((groups, wide, seqs, rows, cols), jnp.bfloat16),
            jax.ShapeDtypeStruct((SLABS, pairs, chunk, SLAB), jnp.int32),
        ),
        grid_spec=pltpu.PrefetchScalarGridSpec(
            num_scalar_prefetch=3,
            grid=(seqs,),
            in_specs=[pl.BlockSpec(memory_space=pl.ANY)] * 3,
            out_specs=(
                pl.BlockSpec((groups, wide, 1, rows, cols), lambda s, *_: (0, 0, s, 0, 0)),
                pl.BlockSpec(memory_space=pl.ANY),
            ),
            scratch_shapes=[
                pltpu.VMEM((blocks, rank, outs // blocks), jnp.bfloat16),
                pltpu.VMEM((blocks, toks, outs // blocks), jnp.bfloat16),
                pltpu.VMEM((blocks, toks, width // blocks), jnp.bfloat16),
                pltpu.VMEM((CB, SLAB), jnp.int32),
                pltpu.SMEM((cols // CB,), jnp.int32),
                pltpu.VMEM((EARLY, pairs, chunk, SLAB), jnp.int32),
                pltpu.SemaphoreType.DMA((3, blocks)),
                pltpu.SemaphoreType.DMA((EARLY,)),
            ],
        ),
        name="seq_grads",
    )(lengths, seeds, grp, adapter_up_factor.T, output_gradient, hidden)


def fill_positions(pos_ref):
    pos_ref[...] = (
        lax.broadcasted_iota(jnp.int32, pos_ref.shape, 0) * ROW
        + lax.broadcasted_iota(jnp.int32, pos_ref.shape, 1) * FEAT
    )


BLOCK = CB * ROW
SPAN = (CB - 1) * ROW + (K - 1) * FEAT
EDGE = 2**31 - SPAN


def fill_turns(turn_ref, seeds_ref, first_row, rows):
    for pos in range(turn_ref.shape[0]):
        short = EDGE - ((seeds_ref[pos] + first_row * BLOCK) & LOW31)
        turn_ref[pos] = lax.div(jnp.maximum(short + (BLOCK - 1), 0), jnp.int32(BLOCK)) + 2


def slot_row(turn, slot, rows):
    if rows & (rows - 1) == 0:
        return (turn + slot) & (rows - 1)
    return lax.rem(turn + slot, jnp.int32(rows))


def slot_wraps(slot, rows):
    return slot >= rows - 2 or rows * BLOCK + SPAN > 2**31


def slab_pairs(pos_ref, seeds_ref, turn_ref, first_row, slab, rows, halves, chunk):
    def top_of(entry):
        slot, half = divmod(entry, halves)
        return slot_tile(pos_ref, seeds_ref, turn_ref, first_row, slab * SLAB, slot, half, chunk // CB, rows)

    for pair in range(rows * halves // 2):
        yield pair, top_of(2 * pair) | shift_down(top_of(2 * pair + 1), 17)


def slot_tile(pos_ref, seeds_ref, turn_ref, first_row, feat, slot, half, parts, rows):
    tile = []
    for part in range(half * parts, (half + 1) * parts):
        row = first_row + slot_row(turn_ref[part], slot, rows)
        tile.append(pos_ref[...] + ((seeds_ref[part] + row * BLOCK + feat * FEAT) & LOW31))
    return mixed(jnp.concatenate(tile, axis=0) if parts > 1 else tile[0], slot_wraps(slot, rows))


def presign_kernel(seeds_ref, grp_ref, early_ref, out_ref, pos_ref, turn_ref, *, rows, halves):
    slab = pl.program_id(0)
    first_row = grp_ref[0] * rows
    chunk = out_ref.shape[2]

    @pl.when(slab == 0)
    def _():
        fill_positions(pos_ref)
        fill_turns(turn_ref, seeds_ref, first_row, rows)

    for pair, word in slab_pairs(pos_ref, seeds_ref, turn_ref, first_row, EARLY + slab, rows, halves, chunk):
        out_ref[0, pair] = word


def presign(seeds, grp, held, rows, cols):
    chunk = min(256, cols)
    chunks = rows * cols // chunk
    return pl.pallas_call(
        functools.partial(presign_kernel, rows=rows, halves=cols // chunk),
        out_shape=jax.ShapeDtypeStruct((SLABS, chunks // 2, chunk, SLAB), jnp.int32),
        grid_spec=pltpu.PrefetchScalarGridSpec(
            num_scalar_prefetch=2,
            grid=(SLABS - EARLY,),
            in_specs=[pl.BlockSpec(memory_space=pl.ANY)],
            out_specs=pl.BlockSpec((1, chunks // 2, chunk, SLAB), lambda i, s, g: (EARLY + i, 0, 0, 0)),
            scratch_shapes=[pltpu.VMEM((CB, SLAB), jnp.int32), pltpu.SMEM((cols // CB,), jnp.int32)],
        ),
        cost_estimate=pl.CostEstimate(
            flops=SLABS * SLAB * rows * cols * 10, bytes_accessed=SLABS * SLAB * rows * cols * 2, transcendentals=0
        ),
        input_output_aliases={2: 0},
        name="presign",
    )(seeds, grp, held)


def project_kernel(
    seeds_ref,
    grp_ref,
    grad_ref,
    first_ref,
    second_ref,
    held_ref,
    last_ref,
    out_ref,
    feat_ref,
    wide_ref,
    upd_ref,
    sum_ref,
    pos_ref,
    turn_ref,
):
    step = pl.program_id(0)
    seqs, rows, cols = grad_ref.shape
    chunk = upd_ref.shape[2]
    halves = cols // chunk
    parts = chunk // CB
    first_row = grp_ref[0] * rows

    @pl.when(step == 0)
    def _():
        fill_positions(pos_ref)
        fill_turns(turn_ref, seeds_ref, first_row, rows)
        width = min(LANES, cols)

        def update_step(blk, carry):
            at = pl.ds(pl.multiple_of(blk * SEQ_BLOCK, SEQ_BLOCK), SEQ_BLOCK)
            for row in range(0, rows, 8):
                for lane in range(0, cols, LANES):
                    spot = (slice(row, row + 8), slice(lane, lane + width))
                    grad = grad_ref[(at, *spot)].astype(jnp.float32)
                    first_new = 0.9 * first_ref[spot] + 0.1 * grad
                    second_new = 0.999 * second_ref[spot] + 0.001 * grad * grad
                    update = first_new / (jnp.sqrt(second_new) + 1e-08)
                    update = jnp.swapaxes(update, 0, 1).astype(jnp.bfloat16)
                    wide_ref[lane // LANES, row : row + 8, at, :width] = update
            return carry

        lax.fori_loop(0, seqs // SEQ_BLOCK, update_step, 0)
        total = jnp.zeros((seqs, width), jnp.float32)
        lanes = lax.broadcasted_iota(jnp.int32, (seqs, LANES), 1)
        for entry in range(upd_ref.shape[0]):
            slot, half = divmod(entry, halves)
            for lane in range(0, chunk, LANES):
                spot = half * chunk + lane
                upd = wide_ref[spot // LANES, slot_row(turn_ref[spot // CB], slot, rows)]
                for pos in range(CB, width, CB):
                    row = slot_row(turn_ref[(spot + pos) // CB], slot, rows)
                    upd = jnp.where(lanes < pos, upd, wide_ref[spot // LANES, row])
                upd = upd[:, :width]
                upd_ref[entry, :, lane : lane + width] = upd
                total += upd.astype(jnp.float32)
        sum_ref[...] = jnp.broadcast_to(jnp.sum(total, axis=1, keepdims=True), sum_ref.shape)

    feats = feat_ref.shape[0] // seqs
    held_feats = SLABS * SLAB
    start = jnp.broadcast_to(sum_ref[:, :1], (seqs, KT))

    def put(first_feat, acc):
        for part in range(acc.shape[1] // LANES):
            feat_ref[pl.ds(first_feat // LANES + part, seqs, stride=feats), :] = acc[:, part * LANES : (part + 1) * LANES]

    def tile_step(slabs):
        feat = held_feats + step * KT
        accs = [start] + [start[:, :SLAB]] * len(slabs)
        for entry in range(upd_ref.shape[0]):
            slot, half = divmod(entry, halves)
            tops = [slot_tile(pos_ref, seeds_ref, turn_ref, first_row, feat, slot, half, parts, rows)]
            words = [ref[0, entry // 2] for ref, _ in slabs]
            tops += [word << 17 if entry % 2 else word for word in words]
            for pos, top in enumerate(tops):
                accs[pos] += jnp.dot(upd_ref[entry], sign_weights(top), preferred_element_type=jnp.float32)
        put(feat, accs[0])
        for (_, slab), acc in zip(slabs, accs[1:]):
            put(slab * SLAB, acc)

    steps = pl.num_programs(0)
    twice = SLABS - steps
    pl.when(step < steps - twice)(lambda: tile_step([(held_ref, step)]))
    pl.when(step >= steps - twice)(lambda: tile_step([(held_ref, step), (last_ref, step + twice)]))

    @pl.when(step == steps - 1)
    def _():
        out_ref[...] = feat_ref[...].astype(out_ref.dtype)


def project(grads, first, second, seeds, grp, held):
    seqs, rows, cols = grads.shape
    chunk = min(256, cols)
    chunks = rows * cols // chunk
    feats = K // LANES
    steps = (K - SLABS * SLAB) // KT
    return pl.pallas_call(
        project_kernel,
        out_shape=jax.ShapeDtypeStruct((seqs * feats, LANES), jnp.bfloat16),
        grid_spec=pltpu.PrefetchScalarGridSpec(
            num_scalar_prefetch=2,
            grid=(steps,),
            in_specs=[
                pl.BlockSpec(memory_space=pltpu.VMEM),
                pl.BlockSpec((rows, cols), lambda i, s, g: (g[0], 0)),
                pl.BlockSpec((rows, cols), lambda i, s, g: (g[0], 0)),
                pl.BlockSpec((1, chunks // 2, chunk, SLAB), lambda i, s, g: (i, 0, 0, 0)),
                pl.BlockSpec(
                    (1, chunks // 2, chunk, SLAB),
                    lambda i, s, g: (jnp.maximum(i + SLABS - steps, steps), 0, 0, 0),
                ),
            ],
            out_specs=pl.BlockSpec((seqs * feats, LANES), lambda i, s, g: (0, 0)),
            scratch_shapes=[
                pltpu.VMEM((seqs * feats, LANES), jnp.float32),
                pltpu.VMEM((pl.cdiv(cols, LANES), rows, seqs, LANES), jnp.bfloat16),
                pltpu.VMEM((chunks, seqs, chunk), jnp.bfloat16),
                pltpu.VMEM((seqs, LANES), jnp.float32),
                pltpu.VMEM((CB, KT), jnp.int32),
                pltpu.SMEM((cols // CB,), jnp.int32),
            ],
        ),
        compiler_params=pltpu.CompilerParams(vmem_limit_bytes=PROJECT_VMEM),
        name="project",
    )(seeds, grp, grads, first, second, held, held)


def finish_kernel(partial_ref, out_ref):
    total = jnp.sum(partial_ref[...].astype(jnp.float32), axis=0)
    mean = jnp.sum(total * total, axis=(1, 2), keepdims=True) / K
    out_ref[...] = total * lax.rsqrt(mean + 1e-06)


def shards(
    hidden,
    output_gradient,
    adapter_up_factor,
    first_moment_estimate,
    second_moment_estimate,
    lengths,
    seeds,
):
    groups, wide = lax.axis_size("grp"), lax.axis_size("wide")
    devices = groups * wide
    own_seqs = hidden.shape[0]
    grp = lax.axis_index("grp").astype(jnp.int32).reshape(1)
    grads, held = seq_grads(hidden, output_gradient, adapter_up_factor, lengths, seeds, grp, groups, wide)
    rows, cols = grads.shape[-2:]
    grads = grads.reshape(devices, own_seqs, rows, cols)
    held = presign(seeds, grp, held, rows, cols)
    grads = lax.all_to_all(grads, AXES, 0, 0, tiled=True).reshape(devices * own_seqs, rows, cols)
    grads = pltpu.with_memory_space_constraint(grads, pltpu.VMEM)
    partial = project(grads, first_moment_estimate, second_moment_estimate, seeds, grp, held)
    partial = partial.reshape(devices, own_seqs, K // LANES, LANES)
    partial = lax.all_to_all(partial, AXES, 0, 0, tiled=True)
    out = pl.pallas_call(
        finish_kernel,
        out_shape=jax.ShapeDtypeStruct((own_seqs, K // LANES, LANES), jnp.float32),
        name="finish",
    )(partial)
    return out.reshape(own_seqs, K)


def solution(mesh):
    placed = (
        P(AXES, None, None),
        P(AXES, None, None),
        P(),
        P(None, "wide"),
        P(None, "wide"),
        P(AXES),
        P("wide"),
    )
    with jax.sharding.use_abstract_mesh(mesh.abstract_mesh):
        return jax.shard_map(shards, mesh=mesh, in_specs=placed, out_specs=P(AXES, None), check_vma=False)
```

```python
import functools
import jax
import jax.numpy as jnp
from jax import lax
from jax.experimental import pallas as pl
from jax.experimental.pallas import tpu as pltpu
from jax.sharding import PartitionSpec as P

K = 4096
CB = 64
MUL = 73244475
TOP = (((MUL + 65536) << 15) + 2**31) % 2**32 - 2**31
LOW31 = 2147483647
ROW = 1000003
FEAT = 7919
AXES = ("grp", "wide")
LANES = 128
KT = 256
SLAB = 128
SLABS = 12
EARLY = 2
SEQ_BLOCK = 16
PROJECT_VMEM = 36 << 20


def shift_down(bits, places):
    return lax.shift_right_logical(bits, jnp.int32(places))


def mixed(hashed, wraps):
    top = shift_down(hashed, 16)
    if wraps:
        top = top & 32767
    hashed = (hashed ^ top) * MUL
    return (hashed ^ (shift_down(hashed, 16) & 32767)) * jnp.int32(TOP)


def sign_weights(top):
    return jnp.where(top < 0, -2.0, 0.0).astype(jnp.bfloat16)


def grad_kernel(
    lens_ref,
    seeds_ref,
    grp_ref,
    up_any,
    outg_any,
    hid_any,
    out_ref,
    held_any,
    up_ref,
    outg_ref,
    hid_ref,
    pos_ref,
    turn_ref,
    held_ref,
    sems,
    held_sems,
    *,
    single,
):
    seq = pl.program_id(0)
    blocks, toks, outs = outg_ref.shape
    width = hid_ref.shape[2]
    groups, wide, _, rows, cols = out_ref.shape
    chunk = held_ref.shape[2]
    first_row = grp_ref[0] * rows

    def loads(blk):
        return (
            pltpu.make_async_copy(up_any.at[:, pl.ds(blk * outs, outs)], up_ref.at[blk], sems.at[0, blk]),
            pltpu.make_async_copy(outg_any.at[seq, :, pl.ds(blk * outs, outs)], outg_ref.at[blk], sems.at[1, blk]),
            pltpu.make_async_copy(hid_any.at[seq, :, pl.ds(blk * width, width)], hid_ref.at[blk], sems.at[2, blk]),
        )

    copies = [loads(blk) for blk in range(blocks)]
    for load_up, load_outg, _ in copies:
        load_up.start()
        load_outg.start()
    for _, _, load_hid in copies:
        load_hid.start()

    pieces = held_ref.shape[1] // blocks

    def held_copy(slab, blk):
        span = pl.ds(blk * pieces, pieces)
        return pltpu.make_async_copy(held_ref.at[slab, span], held_any.at[slab, span], held_sems.at[slab, blk])

    def hold(slab, blk):
        def fill():
            span = range(blk * pieces, (blk + 1) * pieces)
            for pair, word in slab_pairs(pos_ref, seeds_ref, turn_ref, first_row, slab, rows, cols // chunk, chunk, span):
                held_ref[slab, pair] = word
            held_copy(slab, blk).start()

        once(fill)

    def once(task):
        if single:
            task()
        else:
            pl.when(seq == 0)(task)

    def start_hold():
        fill_positions(pos_ref)
        fill_turns(turn_ref, seeds_ref, first_row, rows)

    once(start_hold)
    for slab in range(EARLY):
        for blk in range(blocks):
            hold(slab, blk)
    low = jnp.zeros((toks, up_ref.shape[1]), jnp.float32)
    for blk, (load_up, load_outg, _) in enumerate(copies):
        load_up.wait()
        load_outg.wait()
        low += lax.dot_general(
            outg_ref[blk], up_ref[blk], (((1,), (1,)), ((), ())), preferred_element_type=jnp.float32
        )
    live = lax.broadcasted_iota(jnp.int32, low.shape, 0) < lens_ref[seq]
    low = jnp.where(live, low, 0.0).T.astype(jnp.bfloat16)
    count = lens_ref[seq].astype(jnp.float32)
    for blk, (_, _, load_hid) in enumerate(copies):
        load_hid.wait()
        summed = jnp.dot(low, hid_ref[blk], preferred_element_type=jnp.float32)
        grad = (summed / count).astype(jnp.bfloat16)
        for grp in range(groups):
            for own in range(width // cols):
                out_ref[grp, blk * (width // cols) + own, 0] = grad[
                    grp * rows : (grp + 1) * rows, own * cols : (own + 1) * cols
                ]

    def end_hold():
        for slab in range(EARLY):
            for blk in range(blocks):
                held_copy(slab, blk).wait()

    once(end_hold)


def seq_grads(hidden, output_gradient, adapter_up_factor, lengths, seeds, grp, groups, wide):
    seqs, toks, width = hidden.shape
    outs, rank = adapter_up_factor.shape
    rows, cols = rank // groups, width // wide
    chunk = min(256, cols)
    pairs = rows * cols // chunk // 2
    blocks = 4
    return pl.pallas_call(
        functools.partial(grad_kernel, single=seqs == 1),
        out_shape=(
            jax.ShapeDtypeStruct((groups, wide, seqs, rows, cols), jnp.bfloat16),
            jax.ShapeDtypeStruct((SLABS, pairs, chunk, SLAB), jnp.int32),
        ),
        grid_spec=pltpu.PrefetchScalarGridSpec(
            num_scalar_prefetch=3,
            grid=(seqs,),
            in_specs=[pl.BlockSpec(memory_space=pl.ANY)] * 3,
            out_specs=(
                pl.BlockSpec((groups, wide, 1, rows, cols), lambda s, *_: (0, 0, s, 0, 0)),
                pl.BlockSpec(memory_space=pl.ANY),
            ),
            scratch_shapes=[
                pltpu.VMEM((blocks, rank, outs // blocks), jnp.bfloat16),
                pltpu.VMEM((blocks, toks, outs // blocks), jnp.bfloat16),
                pltpu.VMEM((blocks, toks, width // blocks), jnp.bfloat16),
                pltpu.VMEM((CB, SLAB), jnp.int32),
                pltpu.SMEM((cols // CB,), jnp.int32),
                pltpu.VMEM((EARLY, pairs, chunk, SLAB), jnp.int32),
                pltpu.SemaphoreType.DMA((3, blocks)),
                pltpu.SemaphoreType.DMA((EARLY, blocks)),
            ],
        ),
        name="seq_grads",
    )(lengths, seeds, grp, adapter_up_factor.T, output_gradient, hidden)


def fill_positions(pos_ref):
    pos_ref[...] = (
        lax.broadcasted_iota(jnp.int32, pos_ref.shape, 0) * ROW
        + lax.broadcasted_iota(jnp.int32, pos_ref.shape, 1) * FEAT
    )


BLOCK = CB * ROW
SPAN = (CB - 1) * ROW + (K - 1) * FEAT
EDGE = 2**31 - SPAN


def fill_turns(turn_ref, seeds_ref, first_row, rows):
    for pos in range(turn_ref.shape[0]):
        short = EDGE - ((seeds_ref[pos] + first_row * BLOCK) & LOW31)
        turn_ref[pos] = lax.div(jnp.maximum(short + (BLOCK - 1), 0), jnp.int32(BLOCK)) + 2


def slot_row(turn, slot, rows):
    if rows & (rows - 1) == 0:
        return (turn + slot) & (rows - 1)
    return lax.rem(turn + slot, jnp.int32(rows))


def slot_wraps(slot, rows):
    return slot >= rows - 2 or rows * BLOCK + SPAN > 2**31


def slab_pairs(pos_ref, seeds_ref, turn_ref, first_row, slab, rows, halves, chunk, pairs):
    def top_of(entry):
        slot, half = divmod(entry, halves)
        return slot_tile(pos_ref, seeds_ref, turn_ref, first_row, slab * SLAB, slot, half, chunk // CB, rows)

    for pair in pairs:
        yield pair, top_of(2 * pair) | shift_down(top_of(2 * pair + 1), 17)


def slot_tile(pos_ref, seeds_ref, turn_ref, first_row, feat, slot, half, parts, rows):
    tile = []
    for part in range(half * parts, (half + 1) * parts):
        row = first_row + slot_row(turn_ref[part], slot, rows)
        tile.append(pos_ref[...] + ((seeds_ref[part] + row * BLOCK + feat * FEAT) & LOW31))
    return mixed(jnp.concatenate(tile, axis=0) if parts > 1 else tile[0], slot_wraps(slot, rows))


def presign_kernel(seeds_ref, grp_ref, early_ref, out_ref, pos_ref, turn_ref, *, rows, halves):
    slab = pl.program_id(0)
    first_row = grp_ref[0] * rows
    pairs, chunk = range(out_ref.shape[1]), out_ref.shape[2]

    @pl.when(slab == 0)
    def _():
        fill_positions(pos_ref)
        fill_turns(turn_ref, seeds_ref, first_row, rows)

    for pair, word in slab_pairs(pos_ref, seeds_ref, turn_ref, first_row, EARLY + slab, rows, halves, chunk, pairs):
        out_ref[0, pair] = word


def presign(seeds, grp, held, rows, cols):
    chunk = min(256, cols)
    chunks = rows * cols // chunk
    return pl.pallas_call(
        functools.partial(presign_kernel, rows=rows, halves=cols // chunk),
        out_shape=jax.ShapeDtypeStruct((SLABS, chunks // 2, chunk, SLAB), jnp.int32),
        grid_spec=pltpu.PrefetchScalarGridSpec(
            num_scalar_prefetch=2,
            grid=(SLABS - EARLY,),
            in_specs=[pl.BlockSpec(memory_space=pl.ANY)],
            out_specs=pl.BlockSpec((1, chunks // 2, chunk, SLAB), lambda i, s, g: (EARLY + i, 0, 0, 0)),
            scratch_shapes=[pltpu.VMEM((CB, SLAB), jnp.int32), pltpu.SMEM((cols // CB,), jnp.int32)],
        ),
        cost_estimate=pl.CostEstimate(
            flops=SLABS * SLAB * rows * cols * 10, bytes_accessed=SLABS * SLAB * rows * cols * 2, transcendentals=0
        ),
        input_output_aliases={2: 0},
        name="presign",
    )(seeds, grp, held)


def project_kernel(
    seeds_ref,
    grp_ref,
    grad_ref,
    first_ref,
    second_ref,
    held_any,
    out_ref,
    feat_ref,
    wide_ref,
    upd_ref,
    sum_ref,
    pos_ref,
    turn_ref,
    held_ref,
    held_sems,
):
    step = pl.program_id(0)
    steps = pl.num_programs(0)
    twice = SLABS - steps
    seqs, rows, cols = grad_ref.shape
    chunk = upd_ref.shape[2]
    halves = cols // chunk
    parts = chunk // CB
    first_row = grp_ref[0] * rows

    def held_copy(slab, spot):
        return pltpu.make_async_copy(held_any.at[slab], held_ref.at[spot], held_sems.at[spot])

    @pl.when(step == 0)
    def _():
        for spot in range(2):
            held_copy(spot, spot).start()
        for pos in range(twice):
            held_copy(steps + pos, 2 + pos).start()
        fill_positions(pos_ref)
        fill_turns(turn_ref, seeds_ref, first_row, rows)
        width = min(LANES, cols)

        def update_step(blk, carry):
            at = pl.ds(pl.multiple_of(blk * SEQ_BLOCK, SEQ_BLOCK), SEQ_BLOCK)
            for row in range(0, rows, 8):
                for lane in range(0, cols, LANES):
                    spot = (slice(row, row + 8), slice(lane, lane + width))
                    grad = grad_ref[(at, *spot)].astype(jnp.float32)
                    first_new = 0.9 * first_ref[spot] + 0.1 * grad
                    second_new = 0.999 * second_ref[spot] + 0.001 * grad * grad
                    update = first_new / (jnp.sqrt(second_new) + 1e-08)
                    update = jnp.swapaxes(update, 0, 1).astype(jnp.bfloat16)
                    wide_ref[lane // LANES, row : row + 8, at, :width] = update
            return carry

        lax.fori_loop(0, seqs // SEQ_BLOCK, update_step, 0)
        total = jnp.zeros((seqs, width), jnp.float32)
        lanes = lax.broadcasted_iota(jnp.int32, (seqs, LANES), 1)
        for entry in range(upd_ref.shape[0]):
            slot, half = divmod(entry, halves)
            for lane in range(0, chunk, LANES):
                spot = half * chunk + lane
                upd = wide_ref[spot // LANES, slot_row(turn_ref[spot // CB], slot, rows)]
                for pos in range(CB, width, CB):
                    row = slot_row(turn_ref[(spot + pos) // CB], slot, rows)
                    upd = jnp.where(lanes < pos, upd, wide_ref[spot // LANES, row])
                upd = upd[:, :width]
                upd_ref[entry, :, lane : lane + width] = upd
                total += upd.astype(jnp.float32)
        sum_ref[...] = jnp.broadcast_to(jnp.sum(total, axis=1, keepdims=True), sum_ref.shape)

    feats = feat_ref.shape[0] // seqs
    held_feats = SLABS * SLAB
    start = jnp.broadcast_to(sum_ref[:, :1], (seqs, KT))

    def put(first_feat, acc):
        for part in range(acc.shape[1] // LANES):
            feat_ref[pl.ds(first_feat // LANES + part, seqs, stride=feats), :] = acc[:, part * LANES : (part + 1) * LANES]

    def tile_step(slabs):
        feat = held_feats + step * KT
        accs = [start] + [start[:, :SLAB]] * len(slabs)
        for slab, spot in slabs:
            held_copy(slab, spot).wait()
        for entry in range(upd_ref.shape[0]):
            slot, half = divmod(entry, halves)
            tops = [slot_tile(pos_ref, seeds_ref, turn_ref, first_row, feat, slot, half, parts, rows)]
            words = [held_ref[spot, entry // 2] for _, spot in slabs]
            tops += [word << 17 if entry % 2 else word for word in words]
            for pos, top in enumerate(tops):
                accs[pos] += jnp.dot(upd_ref[entry], sign_weights(top), preferred_element_type=jnp.float32)
        put(feat, accs[0])
        for (slab, _), acc in zip(slabs, accs[1:]):
            put(slab * SLAB, acc)

    spot = lax.rem(step, 2)
    pl.when(step < steps - twice)(lambda: tile_step([(step, spot)]))
    pl.when(step >= steps - twice)(lambda: tile_step([(step, spot), (step + twice, step - (steps - twice) + 2)]))

    @pl.when(step + 2 < steps)
    def _():
        held_copy(step + 2, spot).start()

    @pl.when(step == steps - 1)
    def _():
        out_ref[...] = feat_ref[...].astype(out_ref.dtype)


def project(grads, first, second, seeds, grp, held):
    seqs, rows, cols = grads.shape
    chunk = min(256, cols)
    chunks = rows * cols // chunk
    feats = K // LANES
    steps = (K - SLABS * SLAB) // KT
    return pl.pallas_call(
        project_kernel,
        out_shape=jax.ShapeDtypeStruct((seqs * feats, LANES), jnp.bfloat16),
        grid_spec=pltpu.PrefetchScalarGridSpec(
            num_scalar_prefetch=2,
            grid=(steps,),
            in_specs=[
                pl.BlockSpec(memory_space=pltpu.VMEM),
                pl.BlockSpec((rows, cols), lambda i, s, g: (g[0], 0)),
                pl.BlockSpec((rows, cols), lambda i, s, g: (g[0], 0)),
                pl.BlockSpec(memory_space=pl.ANY),
            ],
            out_specs=pl.BlockSpec((seqs * feats, LANES), lambda i, s, g: (0, 0)),
            scratch_shapes=[
                pltpu.VMEM((seqs * feats, LANES), jnp.float32),
                pltpu.VMEM((pl.cdiv(cols, LANES), rows, seqs, LANES), jnp.bfloat16),
                pltpu.VMEM((chunks, seqs, chunk), jnp.bfloat16),
                pltpu.VMEM((seqs, LANES), jnp.float32),
                pltpu.VMEM((CB, KT), jnp.int32),
                pltpu.SMEM((cols // CB,), jnp.int32),
                pltpu.VMEM((2 + SLABS - steps, chunks // 2, chunk, SLAB), jnp.int32),
                pltpu.SemaphoreType.DMA((2 + SLABS - steps,)),
            ],
        ),
        compiler_params=pltpu.CompilerParams(vmem_limit_bytes=PROJECT_VMEM),
        name="project",
    )(seeds, grp, grads, first, second, held)


def finish_kernel(partial_ref, out_ref):
    total = jnp.sum(partial_ref[...].astype(jnp.float32), axis=0)
    mean = jnp.sum(total * total, axis=(1, 2), keepdims=True) / K
    out_ref[...] = total * lax.rsqrt(mean + 1e-06)


def shards(
    hidden,
    output_gradient,
    adapter_up_factor,
    first_moment_estimate,
    second_moment_estimate,
    lengths,
    seeds,
):
    groups, wide = lax.axis_size("grp"), lax.axis_size("wide")
    devices = groups * wide
    own_seqs = hidden.shape[0]
    grp = lax.axis_index("grp").astype(jnp.int32).reshape(1)
    grads, held = seq_grads(hidden, output_gradient, adapter_up_factor, lengths, seeds, grp, groups, wide)
    rows, cols = grads.shape[-2:]
    grads = grads.reshape(devices, own_seqs, rows, cols)
    held = presign(seeds, grp, held, rows, cols)
    grads = lax.all_to_all(grads, AXES, 0, 0, tiled=True).reshape(devices * own_seqs, rows, cols)
    grads = pltpu.with_memory_space_constraint(grads, pltpu.VMEM)
    partial = project(grads, first_moment_estimate, second_moment_estimate, seeds, grp, held)
    partial = partial.reshape(devices, own_seqs, K // LANES, LANES)
    partial = lax.all_to_all(partial, AXES, 0, 0, tiled=True)
    out = pl.pallas_call(
        finish_kernel,
        out_shape=jax.ShapeDtypeStruct((own_seqs, K // LANES, LANES), jnp.float32),
        name="finish",
    )(partial)
    return out.reshape(own_seqs, K)


def solution(mesh):
    placed = (
        P(AXES, None, None),
        P(AXES, None, None),
        P(),
        P(None, "wide"),
        P(None, "wide"),
        P(AXES),
        P("wide"),
    )
    with jax.sharding.use_abstract_mesh(mesh.abstract_mesh):
        return jax.shard_map(shards, mesh=mesh, in_specs=placed, out_specs=P(AXES, None), check_vma=False)
```

```python
import functools
import jax
import jax.numpy as jnp
from jax import lax
from jax.experimental import pallas as pl
from jax.experimental.pallas import tpu as pltpu
from jax.sharding import PartitionSpec as P

K = 4096
CB = 64
MUL = 73244475
TOP = (((MUL + 65536) << 15) + 2**31) % 2**32 - 2**31
LOW31 = 2147483647
ROW = 1000003
FEAT = 7919
AXES = ("grp", "wide")
LANES = 128
KT = 256
SLAB = 128
SLABS = 12
EARLY = 2
SEQ_BLOCK = 16
PROJECT_VMEM = 36 << 20
FINISH_VMEM = 8 << 20
HALVES = 2


def shift_down(bits, places):
    return lax.shift_right_logical(bits, jnp.int32(places))


def mixed(hashed, wraps):
    top = shift_down(hashed, 16)
    if wraps:
        top = top & 32767
    hashed = (hashed ^ top) * MUL
    return (hashed ^ (shift_down(hashed, 16) & 32767)) * jnp.int32(TOP)


def sign_weights(top):
    return jnp.where(top < 0, -2.0, 0.0).astype(jnp.bfloat16)


def grad_kernel(
    lens_ref,
    seeds_ref,
    grp_ref,
    up_any,
    outg_any,
    hid_any,
    out_ref,
    held_any,
    up_ref,
    outg_ref,
    hid_ref,
    pos_ref,
    turn_ref,
    held_ref,
    sems,
    held_sems,
    *,
    single,
):
    seq = pl.program_id(0)
    blocks, toks, outs = outg_ref.shape
    width = hid_ref.shape[2]
    groups, wide, _, rows, cols = out_ref.shape
    chunk = held_ref.shape[2]
    first_row = grp_ref[0] * rows

    def loads(blk):
        return (
            pltpu.make_async_copy(up_any.at[:, pl.ds(blk * outs, outs)], up_ref.at[blk], sems.at[0, blk]),
            pltpu.make_async_copy(outg_any.at[seq, :, pl.ds(blk * outs, outs)], outg_ref.at[blk], sems.at[1, blk]),
            pltpu.make_async_copy(hid_any.at[seq, :, pl.ds(blk * width, width)], hid_ref.at[blk], sems.at[2, blk]),
        )

    copies = [loads(blk) for blk in range(blocks)]
    for load_up, load_outg, _ in copies:
        load_up.start()
        load_outg.start()
    for _, _, load_hid in copies:
        load_hid.start()

    pieces = held_ref.shape[1] // blocks

    def held_copy(slab, blk):
        span = pl.ds(blk * pieces, pieces)
        return pltpu.make_async_copy(held_ref.at[slab, span], held_any.at[slab, span], held_sems.at[slab, blk])

    def hold(slab, blk):
        def fill():
            span = range(blk * pieces, (blk + 1) * pieces)
            for pair, word in slab_pairs(pos_ref, seeds_ref, turn_ref, first_row, slab, rows, cols // chunk, chunk, span):
                held_ref[slab, pair] = word
            held_copy(slab, blk).start()

        once(fill)

    def once(task):
        if single:
            task()
        else:
            pl.when(seq == 0)(task)

    def start_hold():
        fill_positions(pos_ref)
        fill_turns(turn_ref, seeds_ref, first_row, rows)

    once(start_hold)
    for slab in range(EARLY):
        for blk in range(blocks):
            hold(slab, blk)
    low = jnp.zeros((toks, up_ref.shape[1]), jnp.float32)
    for blk, (load_up, load_outg, _) in enumerate(copies):
        load_up.wait()
        load_outg.wait()
        low += lax.dot_general(
            outg_ref[blk], up_ref[blk], (((1,), (1,)), ((), ())), preferred_element_type=jnp.float32
        )
    live = lax.broadcasted_iota(jnp.int32, low.shape, 0) < lens_ref[seq]
    low = jnp.where(live, low, 0.0).T.astype(jnp.bfloat16)
    count = lens_ref[seq].astype(jnp.float32)
    for blk, (_, _, load_hid) in enumerate(copies):
        load_hid.wait()
        summed = jnp.dot(low, hid_ref[blk], preferred_element_type=jnp.float32)
        grad = (summed / count).astype(jnp.bfloat16)
        for grp in range(groups):
            for own in range(width // cols):
                out_ref[grp, blk * (width // cols) + own, 0] = grad[
                    grp * rows : (grp + 1) * rows, own * cols : (own + 1) * cols
                ]

    def end_hold():
        for slab in range(EARLY):
            for blk in range(blocks):
                held_copy(slab, blk).wait()

    once(end_hold)


def seq_grads(hidden, output_gradient, adapter_up_factor, lengths, seeds, grp, groups, wide):
    seqs, toks, width = hidden.shape
    outs, rank = adapter_up_factor.shape
    rows, cols = rank // groups, width // wide
    chunk = min(256, cols)
    pairs = rows * cols // chunk // 2
    blocks = 4
    return pl.pallas_call(
        functools.partial(grad_kernel, single=seqs == 1),
        out_shape=(
            jax.ShapeDtypeStruct((groups, wide, seqs, rows, cols), jnp.bfloat16),
            jax.ShapeDtypeStruct((SLABS, pairs, chunk, SLAB), jnp.int32),
        ),
        grid_spec=pltpu.PrefetchScalarGridSpec(
            num_scalar_prefetch=3,
            grid=(seqs,),
            in_specs=[pl.BlockSpec(memory_space=pl.ANY)] * 3,
            out_specs=(
                pl.BlockSpec((groups, wide, 1, rows, cols), lambda s, *_: (0, 0, s, 0, 0)),
                pl.BlockSpec(memory_space=pl.ANY),
            ),
            scratch_shapes=[
                pltpu.VMEM((blocks, rank, outs // blocks), jnp.bfloat16),
                pltpu.VMEM((blocks, toks, outs // blocks), jnp.bfloat16),
                pltpu.VMEM((blocks, toks, width // blocks), jnp.bfloat16),
                pltpu.VMEM((CB, SLAB), jnp.int32),
                pltpu.SMEM((cols // CB,), jnp.int32),
                pltpu.VMEM((EARLY, pairs, chunk, SLAB), jnp.int32),
                pltpu.SemaphoreType.DMA((3, blocks)),
                pltpu.SemaphoreType.DMA((EARLY, blocks)),
            ],
        ),
        name="seq_grads",
    )(lengths, seeds, grp, adapter_up_factor.T, output_gradient, hidden)


def fill_positions(pos_ref):
    pos_ref[...] = (
        lax.broadcasted_iota(jnp.int32, pos_ref.shape, 0) * ROW
        + lax.broadcasted_iota(jnp.int32, pos_ref.shape, 1) * FEAT
    )


BLOCK = CB * ROW
SPAN = (CB - 1) * ROW + (K - 1) * FEAT
EDGE = 2**31 - SPAN


def fill_turns(turn_ref, seeds_ref, first_row, rows):
    for pos in range(turn_ref.shape[0]):
        short = EDGE - ((seeds_ref[pos] + first_row * BLOCK) & LOW31)
        turn_ref[pos] = lax.div(jnp.maximum(short + (BLOCK - 1), 0), jnp.int32(BLOCK)) + 2


def slot_row(turn, slot, rows):
    if rows & (rows - 1) == 0:
        return (turn + slot) & (rows - 1)
    return lax.rem(turn + slot, jnp.int32(rows))


def slot_wraps(slot, rows):
    return slot >= rows - 2 or rows * BLOCK + SPAN > 2**31


def slab_pairs(pos_ref, seeds_ref, turn_ref, first_row, slab, rows, halves, chunk, pairs):
    def top_of(entry):
        slot, half = divmod(entry, halves)
        return slot_tile(pos_ref, seeds_ref, turn_ref, first_row, slab * SLAB, slot, half, chunk // CB, rows)

    for pair in pairs:
        yield pair, top_of(2 * pair) | shift_down(top_of(2 * pair + 1), 17)


def slot_tile(pos_ref, seeds_ref, turn_ref, first_row, feat, slot, half, parts, rows):
    tile = []
    for part in range(half * parts, (half + 1) * parts):
        row = first_row + slot_row(turn_ref[part], slot, rows)
        tile.append(pos_ref[...] + ((seeds_ref[part] + row * BLOCK + feat * FEAT) & LOW31))
    return mixed(jnp.concatenate(tile, axis=0) if parts > 1 else tile[0], slot_wraps(slot, rows))


def presign_kernel(seeds_ref, grp_ref, early_ref, out_ref, pos_ref, turn_ref, *, rows, halves):
    slab, side = pl.program_id(0), pl.program_id(1)
    first_row = grp_ref[0] * rows
    pairs, chunk = out_ref.shape[1:3]

    @pl.when((slab == 0) & (side == 0))
    def _():
        fill_positions(pos_ref)
        fill_turns(turn_ref, seeds_ref, first_row, rows)

    def fill(first):
        span = range(first, first + pairs)
        for pair, word in slab_pairs(pos_ref, seeds_ref, turn_ref, first_row, EARLY + slab, rows, halves, chunk, span):
            out_ref[0, pair - first] = word

    for pos in range(HALVES):
        pl.when(side == pos)(functools.partial(fill, pos * pairs))


def presign(seeds, grp, held, rows, cols):
    chunk = min(256, cols)
    chunks = rows * cols // chunk
    return pl.pallas_call(
        functools.partial(presign_kernel, rows=rows, halves=cols // chunk),
        out_shape=jax.ShapeDtypeStruct((SLABS, chunks // 2, chunk, SLAB), jnp.int32),
        grid_spec=pltpu.PrefetchScalarGridSpec(
            num_scalar_prefetch=2,
            grid=(SLABS - EARLY, HALVES),
            in_specs=[pl.BlockSpec(memory_space=pl.ANY)],
            out_specs=pl.BlockSpec((1, chunks // 2 // HALVES, chunk, SLAB), lambda i, j, s, g: (EARLY + i, j, 0, 0)),
            scratch_shapes=[pltpu.VMEM((CB, SLAB), jnp.int32), pltpu.SMEM((cols // CB,), jnp.int32)],
        ),
        cost_estimate=pl.CostEstimate(
            flops=SLABS * SLAB * rows * cols * 10, bytes_accessed=SLABS * SLAB * rows * cols * 2, transcendentals=0
        ),
        input_output_aliases={2: 0},
        name="presign",
    )(seeds, grp, held)


def project_kernel(
    seeds_ref,
    grp_ref,
    grad_ref,
    first_ref,
    second_ref,
    held_any,
    out_ref,
    feat_ref,
    wide_ref,
    upd_ref,
    sum_ref,
    pos_ref,
    turn_ref,
    held_ref,
    held_sems,
):
    step = pl.program_id(0)
    steps = pl.num_programs(0)
    twice = SLABS - steps
    seqs, rows, cols = grad_ref.shape
    chunk = upd_ref.shape[2]
    halves = cols // chunk
    parts = chunk // CB
    first_row = grp_ref[0] * rows

    def held_copy(slab, spot):
        return pltpu.make_async_copy(held_any.at[slab], held_ref.at[spot], held_sems.at[spot])

    @pl.when(step == 0)
    def _():
        for spot in range(2):
            held_copy(spot, spot).start()
        for pos in range(twice):
            held_copy(steps + pos, 2 + pos).start()
        fill_positions(pos_ref)
        fill_turns(turn_ref, seeds_ref, first_row, rows)
        width = min(LANES, cols)

        def update_step(blk, carry):
            at = pl.ds(pl.multiple_of(blk * SEQ_BLOCK, SEQ_BLOCK), SEQ_BLOCK)
            for row in range(0, rows, 8):
                for lane in range(0, cols, LANES):
                    spot = (slice(row, row + 8), slice(lane, lane + width))
                    grad = grad_ref[(at, *spot)].astype(jnp.float32)
                    first_new = 0.9 * first_ref[spot] + 0.1 * grad
                    second_new = 0.999 * second_ref[spot] + 0.001 * grad * grad
                    update = first_new / (jnp.sqrt(second_new) + 1e-08)
                    update = jnp.swapaxes(update, 0, 1).astype(jnp.bfloat16)
                    wide_ref[lane // LANES, row : row + 8, at, :width] = update
            return carry

        lax.fori_loop(0, seqs // SEQ_BLOCK, update_step, 0)
        total = jnp.zeros((seqs, width), jnp.float32)
        lanes = lax.broadcasted_iota(jnp.int32, (seqs, LANES), 1)
        for entry in range(upd_ref.shape[0]):
            slot, half = divmod(entry, halves)
            for lane in range(0, chunk, LANES):
                spot = half * chunk + lane
                upd = wide_ref[spot // LANES, slot_row(turn_ref[spot // CB], slot, rows)]
                for pos in range(CB, width, CB):
                    row = slot_row(turn_ref[(spot + pos) // CB], slot, rows)
                    upd = jnp.where(lanes < pos, upd, wide_ref[spot // LANES, row])
                upd = upd[:, :width]
                upd_ref[entry, :, lane : lane + width] = upd
                total += upd.astype(jnp.float32)
        sum_ref[...] = jnp.broadcast_to(jnp.sum(total, axis=1, keepdims=True), sum_ref.shape)

    feats = feat_ref.shape[0] // seqs
    held_feats = SLABS * SLAB
    start = jnp.broadcast_to(sum_ref[:, :1], (seqs, KT))

    def put(first_feat, acc):
        for part in range(acc.shape[1] // LANES):
            feat_ref[pl.ds(first_feat // LANES + part, seqs, stride=feats), :] = acc[:, part * LANES : (part + 1) * LANES]

    def tile_step(slabs):
        feat = held_feats + step * KT
        accs = [start] + [start[:, :SLAB]] * len(slabs)
        for slab, spot in slabs:
            held_copy(slab, spot).wait()
        for entry in range(upd_ref.shape[0]):
            slot, half = divmod(entry, halves)
            tops = [slot_tile(pos_ref, seeds_ref, turn_ref, first_row, feat, slot, half, parts, rows)]
            words = [held_ref[spot, entry // 2] for _, spot in slabs]
            tops += [word << 17 if entry % 2 else word for word in words]
            for pos, top in enumerate(tops):
                accs[pos] += jnp.dot(upd_ref[entry], sign_weights(top), preferred_element_type=jnp.float32)
        put(feat, accs[0])
        for (slab, _), acc in zip(slabs, accs[1:]):
            put(slab * SLAB, acc)

    spot = lax.rem(step, 2)
    pl.when(step < steps - twice)(lambda: tile_step([(step, spot)]))
    pl.when(step >= steps - twice)(lambda: tile_step([(step, spot), (step + twice, step - (steps - twice) + 2)]))

    @pl.when(step + 2 < steps)
    def _():
        held_copy(step + 2, spot).start()

    @pl.when(step == steps - 1)
    def _():
        out_ref[...] = feat_ref[...].astype(out_ref.dtype)


def project(grads, first, second, seeds, grp, held):
    seqs, rows, cols = grads.shape
    chunk = min(256, cols)
    chunks = rows * cols // chunk
    feats = K // LANES
    steps = (K - SLABS * SLAB) // KT
    return pl.pallas_call(
        project_kernel,
        out_shape=jax.ShapeDtypeStruct((seqs * feats, LANES), jnp.bfloat16),
        grid_spec=pltpu.PrefetchScalarGridSpec(
            num_scalar_prefetch=2,
            grid=(steps,),
            in_specs=[
                pl.BlockSpec(memory_space=pltpu.VMEM),
                pl.BlockSpec((rows, cols), lambda i, s, g: (g[0], 0)),
                pl.BlockSpec((rows, cols), lambda i, s, g: (g[0], 0)),
                pl.BlockSpec(memory_space=pl.ANY),
            ],
            out_specs=pl.BlockSpec((seqs * feats, LANES), lambda i, s, g: (0, 0)),
            scratch_shapes=[
                pltpu.VMEM((seqs * feats, LANES), jnp.float32),
                pltpu.VMEM((pl.cdiv(cols, LANES), rows, seqs, LANES), jnp.bfloat16),
                pltpu.VMEM((chunks, seqs, chunk), jnp.bfloat16),
                pltpu.VMEM((seqs, LANES), jnp.float32),
                pltpu.VMEM((CB, KT), jnp.int32),
                pltpu.SMEM((cols // CB,), jnp.int32),
                pltpu.VMEM((2 + SLABS - steps, chunks // 2, chunk, SLAB), jnp.int32),
                pltpu.SemaphoreType.DMA((2 + SLABS - steps,)),
            ],
        ),
        compiler_params=pltpu.CompilerParams(vmem_limit_bytes=PROJECT_VMEM),
        name="project",
    )(seeds, grp, grads, first, second, held)


def finish_kernel(partial_ref, out_ref):
    total = jnp.sum(partial_ref[...].astype(jnp.float32), axis=0)
    mean = jnp.sum(total * total, axis=(1, 2), keepdims=True) / K
    out_ref[...] = total * lax.rsqrt(mean + 1e-06)


def shards(
    hidden,
    output_gradient,
    adapter_up_factor,
    first_moment_estimate,
    second_moment_estimate,
    lengths,
    seeds,
):
    groups, wide = lax.axis_size("grp"), lax.axis_size("wide")
    devices = groups * wide
    own_seqs = hidden.shape[0]
    grp = lax.axis_index("grp").astype(jnp.int32).reshape(1)
    grads, held = seq_grads(hidden, output_gradient, adapter_up_factor, lengths, seeds, grp, groups, wide)
    rows, cols = grads.shape[-2:]
    grads = grads.reshape(devices, own_seqs, rows, cols)
    held = presign(seeds, grp, held, rows, cols)
    grads = lax.all_to_all(grads, AXES, 0, 0, tiled=True).reshape(devices * own_seqs, rows, cols)
    grads = pltpu.with_memory_space_constraint(grads, pltpu.VMEM)
    partial = project(grads, first_moment_estimate, second_moment_estimate, seeds, grp, held)
    partial = partial.reshape(devices, own_seqs, K // LANES, LANES)
    partial = lax.all_to_all(partial, AXES, 0, 0, tiled=True)
    partial = pltpu.with_memory_space_constraint(partial, pltpu.VMEM)
    out = pl.pallas_call(
        finish_kernel,
        out_shape=jax.ShapeDtypeStruct((own_seqs, K // LANES, LANES), jnp.float32),
        in_specs=[pl.BlockSpec(memory_space=pltpu.VMEM)],
        compiler_params=pltpu.CompilerParams(vmem_limit_bytes=FINISH_VMEM),
        name="finish",
    )(partial)
    return out.reshape(own_seqs, K)


def solution(mesh):
    placed = (
        P(AXES, None, None),
        P(AXES, None, None),
        P(),
        P(None, "wide"),
        P(None, "wide"),
        P(AXES),
        P("wide"),
    )
    with jax.sharding.use_abstract_mesh(mesh.abstract_mesh):
        return jax.shard_map(shards, mesh=mesh, in_specs=placed, out_specs=P(AXES, None), check_vma=False)
```

```python
import functools
import jax
import jax.numpy as jnp
from jax import lax
from jax.experimental import pallas as pl
from jax.experimental.pallas import tpu as pltpu
from jax.sharding import PartitionSpec as P

K = 4096
CB = 64
MUL = 73244475
TOP = (((MUL + 65536) << 15) + 2**31) % 2**32 - 2**31
LOW31 = 2147483647
ROW = 1000003
FEAT = 7919
AXES = ("grp", "wide")
LANES = 128
KT = 256
SLAB = 128
SLABS = 12
EARLY = 2
SEQ_BLOCK = 16
PROJECT_VMEM = 61 << 20
FINISH_VMEM = 8 << 20
FAR = SLABS - EARLY
QUAD_BITS = (1 << 14) - (1 << 31)


def shift_down(bits, places):
    return lax.shift_right_logical(bits, jnp.int32(places))


def mixed(hashed, wraps):
    top = shift_down(hashed, 16)
    if wraps:
        top = top & 32767
    hashed = (hashed ^ top) * MUL
    return (hashed ^ (shift_down(hashed, 16) & 32767)) * jnp.int32(TOP)


def sign_weights(top):
    return jnp.where(top < 0, -2.0, 0.0).astype(jnp.bfloat16)


def grad_kernel(
    lens_ref,
    seeds_ref,
    grp_ref,
    up_any,
    outg_any,
    hid_any,
    out_ref,
    held_any,
    up_ref,
    outg_ref,
    hid_ref,
    pos_ref,
    turn_ref,
    held_ref,
    sems,
    held_sems,
    *,
    single,
):
    seq = pl.program_id(0)
    blocks, toks, outs = outg_ref.shape
    width = hid_ref.shape[2]
    groups, wide, _, rows, cols = out_ref.shape
    chunk = held_ref.shape[2]
    first_row = grp_ref[0] * rows

    def loads(blk):
        return (
            pltpu.make_async_copy(up_any.at[:, pl.ds(blk * outs, outs)], up_ref.at[blk], sems.at[0, blk]),
            pltpu.make_async_copy(outg_any.at[seq, :, pl.ds(blk * outs, outs)], outg_ref.at[blk], sems.at[1, blk]),
            pltpu.make_async_copy(hid_any.at[seq, :, pl.ds(blk * width, width)], hid_ref.at[blk], sems.at[2, blk]),
        )

    copies = [loads(blk) for blk in range(blocks)]
    for load_up, load_outg, _ in copies:
        load_up.start()
        load_outg.start()
    for _, _, load_hid in copies:
        load_hid.start()

    pieces = held_ref.shape[1] // blocks

    def held_copy(slab, blk):
        span = pl.ds(blk * pieces, pieces)
        return pltpu.make_async_copy(held_ref.at[slab, span], held_any.at[slab, span], held_sems.at[slab, blk])

    def hold(slab, blk):
        def fill():
            span = range(blk * pieces, (blk + 1) * pieces)
            halves = cols // chunk
            quads = slab_words(pos_ref, seeds_ref, turn_ref, first_row, FAR + slab, rows, halves, chunk, span, 4)
            for quad, word in quads:
                held_ref[slab, quad] = word
            held_copy(slab, blk).start()

        once(fill)

    def once(task):
        if single:
            task()
        else:
            pl.when(seq == 0)(task)

    def start_hold():
        fill_positions(pos_ref)
        fill_turns(turn_ref, seeds_ref, first_row, rows)

    once(start_hold)
    for slab in range(EARLY):
        for blk in range(blocks):
            hold(slab, blk)
    low = jnp.zeros((toks, up_ref.shape[1]), jnp.float32)
    for blk, (load_up, load_outg, _) in enumerate(copies):
        load_up.wait()
        load_outg.wait()
        low += lax.dot_general(
            outg_ref[blk], up_ref[blk], (((1,), (1,)), ((), ())), preferred_element_type=jnp.float32
        )
    live = lax.broadcasted_iota(jnp.int32, low.shape, 0) < lens_ref[seq]
    low = jnp.where(live, low, 0.0).T.astype(jnp.bfloat16)
    count = lens_ref[seq].astype(jnp.float32)
    for blk, (_, _, load_hid) in enumerate(copies):
        load_hid.wait()
        summed = jnp.dot(low, hid_ref[blk], preferred_element_type=jnp.float32)
        grad = (summed / count).astype(jnp.bfloat16)
        for grp in range(groups):
            for own in range(width // cols):
                out_ref[grp, blk * (width // cols) + own, 0] = grad[
                    grp * rows : (grp + 1) * rows, own * cols : (own + 1) * cols
                ]

    def end_hold():
        for slab in range(EARLY):
            for blk in range(blocks):
                held_copy(slab, blk).wait()

    once(end_hold)


def seq_grads(hidden, output_gradient, adapter_up_factor, lengths, seeds, grp, groups, wide):
    seqs, toks, width = hidden.shape
    outs, rank = adapter_up_factor.shape
    rows, cols = rank // groups, width // wide
    chunk = min(256, cols)
    quads = rows * cols // chunk // 4
    blocks = 4
    return pl.pallas_call(
        functools.partial(grad_kernel, single=seqs == 1),
        out_shape=(
            jax.ShapeDtypeStruct((groups, wide, seqs, rows, cols), jnp.bfloat16),
            jax.ShapeDtypeStruct((EARLY, quads, chunk, SLAB), jnp.int32),
        ),
        grid_spec=pltpu.PrefetchScalarGridSpec(
            num_scalar_prefetch=3,
            grid=(seqs,),
            in_specs=[pl.BlockSpec(memory_space=pl.ANY)] * 3,
            out_specs=(
                pl.BlockSpec((groups, wide, 1, rows, cols), lambda s, *_: (0, 0, s, 0, 0)),
                pl.BlockSpec(memory_space=pl.ANY),
            ),
            scratch_shapes=[
                pltpu.VMEM((blocks, rank, outs // blocks), jnp.bfloat16),
                pltpu.VMEM((blocks, toks, outs // blocks), jnp.bfloat16),
                pltpu.VMEM((blocks, toks, width // blocks), jnp.bfloat16),
                pltpu.VMEM((CB, SLAB), jnp.int32),
                pltpu.SMEM((cols // CB,), jnp.int32),
                pltpu.VMEM((EARLY, quads, chunk, SLAB), jnp.int32),
                pltpu.SemaphoreType.DMA((3, blocks)),
                pltpu.SemaphoreType.DMA((EARLY, blocks)),
            ],
        ),
        name="seq_grads",
    )(lengths, seeds, grp, adapter_up_factor.T, output_gradient, hidden)


def fill_positions(pos_ref):
    pos_ref[...] = (
        lax.broadcasted_iota(jnp.int32, pos_ref.shape, 0) * ROW
        + lax.broadcasted_iota(jnp.int32, pos_ref.shape, 1) * FEAT
    )


BLOCK = CB * ROW
SPAN = (CB - 1) * ROW + (K - 1) * FEAT
EDGE = 2**31 - SPAN


def fill_turns(turn_ref, seeds_ref, first_row, rows):
    for pos in range(turn_ref.shape[0]):
        short = EDGE - ((seeds_ref[pos] + first_row * BLOCK) & LOW31)
        turn_ref[pos] = lax.div(jnp.maximum(short + (BLOCK - 1), 0), jnp.int32(BLOCK)) + 2


def slot_row(turn, slot, rows):
    if rows & (rows - 1) == 0:
        return (turn + slot) & (rows - 1)
    return lax.rem(turn + slot, jnp.int32(rows))


def slot_wraps(slot, rows):
    return slot >= rows - 2 or rows * BLOCK + SPAN > 2**31


def slab_words(pos_ref, seeds_ref, turn_ref, first_row, slab, rows, halves, chunk, words, per_word):
    def top_of(entry):
        slot, half = divmod(entry, halves)
        return slot_tile(pos_ref, seeds_ref, turn_ref, first_row, slab * SLAB, slot, half, chunk // CB, rows)

    def pair_of(entry):
        return top_of(entry) | shift_down(top_of(entry + 1), 17)

    for word in words:
        if per_word == 2:
            yield word, pair_of(2 * word)
        else:
            yield word, (pair_of(4 * word) & QUAD_BITS) | shift_down(pair_of(4 * word + 2) & QUAD_BITS, 1)


def entry_top(words, entry, per_word):
    place = (0, 17, 1, 18)[entry % per_word]
    return words << place if place else words


def slot_tile(pos_ref, seeds_ref, turn_ref, first_row, feat, slot, half, parts, rows):
    tile = []
    for part in range(half * parts, (half + 1) * parts):
        row = first_row + slot_row(turn_ref[part], slot, rows)
        tile.append(pos_ref[...] + ((seeds_ref[part] + row * BLOCK + feat * FEAT) & LOW31))
    return mixed(jnp.concatenate(tile, axis=0) if parts > 1 else tile[0], slot_wraps(slot, rows))


def presign_kernel(seeds_ref, grp_ref, out_ref, pos_ref, turn_ref, *, rows, halves):
    slab = pl.program_id(0)
    first_row = grp_ref[0] * rows
    pairs, chunk = range(out_ref.shape[1]), out_ref.shape[2]

    @pl.when(slab == 0)
    def _():
        fill_positions(pos_ref)
        fill_turns(turn_ref, seeds_ref, first_row, rows)

    for pair, word in slab_words(pos_ref, seeds_ref, turn_ref, first_row, slab, rows, halves, chunk, pairs, 2):
        out_ref[0, pair] = word


def presign(seeds, grp, rows, cols):
    chunk = min(256, cols)
    chunks = rows * cols // chunk
    return pl.pallas_call(
        functools.partial(presign_kernel, rows=rows, halves=cols // chunk),
        out_shape=jax.ShapeDtypeStruct((FAR, chunks // 2, chunk, SLAB), jnp.int32),
        grid_spec=pltpu.PrefetchScalarGridSpec(
            num_scalar_prefetch=2,
            grid=(FAR,),
            out_specs=pl.BlockSpec((1, chunks // 2, chunk, SLAB), lambda i, s, g: (i, 0, 0, 0)),
            scratch_shapes=[pltpu.VMEM((CB, SLAB), jnp.int32), pltpu.SMEM((cols // CB,), jnp.int32)],
        ),
        cost_estimate=pl.CostEstimate(
            flops=FAR * SLAB * rows * cols * 10, bytes_accessed=FAR * SLAB * rows * cols * 2, transcendentals=0
        ),
        name="presign",
    )(seeds, grp)


def project_kernel(
    seeds_ref,
    grp_ref,
    grad_ref,
    first_ref,
    second_ref,
    held_any,
    early_any,
    out_ref,
    feat_ref,
    wide_ref,
    upd_ref,
    sum_ref,
    pos_ref,
    turn_ref,
    held_ref,
    early_ref,
    held_sems,
    early_sems,
):
    step = pl.program_id(0)
    steps = pl.num_programs(0)
    seqs, rows, cols = grad_ref.shape
    chunk = upd_ref.shape[2]
    halves = cols // chunk
    parts = chunk // CB
    first_row = grp_ref[0] * rows

    def held_copy(slab, spot):
        return pltpu.make_async_copy(held_any.at[slab], held_ref.at[spot], held_sems.at[spot])

    def early_copy(slab):
        return pltpu.make_async_copy(early_any.at[slab], early_ref.at[slab], early_sems.at[slab])

    @pl.when(step == 0)
    def _():
        for spot in range(2):
            held_copy(spot, spot).start()
        for slab in range(EARLY):
            early_copy(slab).start()
        fill_positions(pos_ref)
        fill_turns(turn_ref, seeds_ref, first_row, rows)
        width = min(LANES, cols)

        def update_step(blk, carry):
            at = pl.ds(pl.multiple_of(blk * SEQ_BLOCK, SEQ_BLOCK), SEQ_BLOCK)
            for row in range(0, rows, 8):
                for lane in range(0, cols, LANES):
                    spot = (slice(row, row + 8), slice(lane, lane + width))
                    grad = grad_ref[(at, *spot)].astype(jnp.float32)
                    first_new = 0.9 * first_ref[spot] + 0.1 * grad
                    second_new = 0.999 * second_ref[spot] + 0.001 * grad * grad
                    update = first_new / (jnp.sqrt(second_new) + 1e-08)
                    update = jnp.swapaxes(update, 0, 1).astype(jnp.bfloat16)
                    wide_ref[lane // LANES, row : row + 8, at, :width] = update
            return carry

        lax.fori_loop(0, seqs // SEQ_BLOCK, update_step, 0)
        total = jnp.zeros((seqs, width), jnp.float32)
        lanes = lax.broadcasted_iota(jnp.int32, (seqs, LANES), 1)
        for entry in range(upd_ref.shape[0]):
            slot, half = divmod(entry, halves)
            for lane in range(0, chunk, LANES):
                spot = half * chunk + lane
                upd = wide_ref[spot // LANES, slot_row(turn_ref[spot // CB], slot, rows)]
                for pos in range(CB, width, CB):
                    row = slot_row(turn_ref[(spot + pos) // CB], slot, rows)
                    upd = jnp.where(lanes < pos, upd, wide_ref[spot // LANES, row])
                upd = upd[:, :width]
                upd_ref[entry, :, lane : lane + width] = upd
                total += upd.astype(jnp.float32)
        sum_ref[...] = jnp.broadcast_to(jnp.sum(total, axis=1, keepdims=True), sum_ref.shape)

    feats = feat_ref.shape[0] // seqs
    held_feats = SLABS * SLAB
    start = jnp.broadcast_to(sum_ref[:, :1], (seqs, KT))

    def put(first_feat, acc):
        for part in range(acc.shape[1] // LANES):
            feat_ref[pl.ds(first_feat // LANES + part, seqs, stride=feats), :] = acc[:, part * LANES : (part + 1) * LANES]

    def tile_step(early):
        feat = held_feats + step * KT
        held_copy(step, spot).wait()
        accs = [start, start[:, :SLAB]]
        if early is not None:
            early_copy(early).wait()
            accs.append(start[:, :SLAB])
        for entry in range(upd_ref.shape[0]):
            slot, half = divmod(entry, halves)
            tops = [slot_tile(pos_ref, seeds_ref, turn_ref, first_row, feat, slot, half, parts, rows)]
            tops.append(entry_top(held_ref[spot, entry // 2], entry, 2))
            if early is not None:
                tops.append(entry_top(early_ref[early, entry // 4], entry, 4))
            for pos, top in enumerate(tops):
                accs[pos] += jnp.dot(upd_ref[entry], sign_weights(top), preferred_element_type=jnp.float32)
        put(feat, accs[0])
        put(step * SLAB, accs[1])
        if early is not None:
            put((FAR + early) * SLAB, accs[2])

    spot = lax.rem(step, 2)
    pl.when(step < steps - EARLY)(lambda: tile_step(None))
    pl.when(step >= steps - EARLY)(lambda: tile_step(step - (steps - EARLY)))

    @pl.when(step + 2 < steps)
    def _():
        held_copy(step + 2, spot).start()

    @pl.when(step == steps - 1)
    def _():
        out_ref[...] = feat_ref[...].astype(out_ref.dtype)


def project(grads, first, second, seeds, grp, held, early):
    seqs, rows, cols = grads.shape
    chunk = min(256, cols)
    chunks = rows * cols // chunk
    feats = K // LANES
    steps = (K - SLABS * SLAB) // KT
    assert steps == FAR
    return pl.pallas_call(
        project_kernel,
        out_shape=jax.ShapeDtypeStruct((seqs * feats, LANES), jnp.bfloat16),
        grid_spec=pltpu.PrefetchScalarGridSpec(
            num_scalar_prefetch=2,
            grid=(steps,),
            in_specs=[
                pl.BlockSpec(memory_space=pltpu.VMEM),
                pl.BlockSpec((rows, cols), lambda i, s, g: (g[0], 0)),
                pl.BlockSpec((rows, cols), lambda i, s, g: (g[0], 0)),
                pl.BlockSpec(memory_space=pl.ANY),
                pl.BlockSpec(memory_space=pl.ANY),
            ],
            out_specs=pl.BlockSpec((seqs * feats, LANES), lambda i, s, g: (0, 0)),
            scratch_shapes=[
                pltpu.VMEM((seqs * feats, LANES), jnp.float32),
                pltpu.VMEM((pl.cdiv(cols, LANES), rows, seqs, LANES), jnp.bfloat16),
                pltpu.VMEM((chunks, seqs, chunk), jnp.bfloat16),
                pltpu.VMEM((seqs, LANES), jnp.float32),
                pltpu.VMEM((CB, KT), jnp.int32),
                pltpu.SMEM((cols // CB,), jnp.int32),
                pltpu.VMEM((2, chunks // 2, chunk, SLAB), jnp.int32),
                pltpu.VMEM((EARLY, chunks // 4, chunk, SLAB), jnp.int32),
                pltpu.SemaphoreType.DMA((2,)),
                pltpu.SemaphoreType.DMA((EARLY,)),
            ],
        ),
        compiler_params=pltpu.CompilerParams(vmem_limit_bytes=PROJECT_VMEM),
        name="project",
    )(seeds, grp, grads, first, second, held, early)


def finish_kernel(partial_ref, out_ref):
    total = jnp.sum(partial_ref[...].astype(jnp.float32), axis=0)
    mean = jnp.sum(total * total, axis=(1, 2), keepdims=True) / K
    out_ref[...] = total * lax.rsqrt(mean + 1e-06)


def shards(
    hidden,
    output_gradient,
    adapter_up_factor,
    first_moment_estimate,
    second_moment_estimate,
    lengths,
    seeds,
):
    groups, wide = lax.axis_size("grp"), lax.axis_size("wide")
    devices = groups * wide
    own_seqs = hidden.shape[0]
    grp = lax.axis_index("grp").astype(jnp.int32).reshape(1)
    grads, early = seq_grads(hidden, output_gradient, adapter_up_factor, lengths, seeds, grp, groups, wide)
    rows, cols = grads.shape[-2:]
    grads = grads.reshape(devices, own_seqs, rows, cols)
    held = presign(seeds, grp, rows, cols)
    grads = lax.all_to_all(grads, AXES, 0, 0, tiled=True).reshape(devices * own_seqs, rows, cols)
    grads = pltpu.with_memory_space_constraint(grads, pltpu.VMEM)
    partial = project(grads, first_moment_estimate, second_moment_estimate, seeds, grp, held, early)
    partial = partial.reshape(devices, own_seqs, K // LANES, LANES)
    partial = lax.all_to_all(partial, AXES, 0, 0, tiled=True)
    partial = pltpu.with_memory_space_constraint(partial, pltpu.VMEM)
    out = pl.pallas_call(
        finish_kernel,
        out_shape=jax.ShapeDtypeStruct((own_seqs, K // LANES, LANES), jnp.float32),
        in_specs=[pl.BlockSpec(memory_space=pltpu.VMEM)],
        compiler_params=pltpu.CompilerParams(vmem_limit_bytes=FINISH_VMEM),
        name="finish",
    )(partial)
    return out.reshape(own_seqs, K)


def solution(mesh):
    placed = (
        P(AXES, None, None),
        P(AXES, None, None),
        P(),
        P(None, "wide"),
        P(None, "wide"),
        P(AXES),
        P("wide"),
    )
    with jax.sharding.use_abstract_mesh(mesh.abstract_mesh):
        return jax.shard_map(shards, mesh=mesh, in_specs=placed, out_specs=P(AXES, None), check_vma=False)
```

```python
import functools
import jax
import jax.numpy as jnp
from jax import lax
from jax.experimental import pallas as pl
from jax.experimental.pallas import tpu as pltpu
from jax.sharding import PartitionSpec as P

K = 4096
CB = 64
MUL = 73244475
TOP = (((MUL + 65536) << 15) + 2**31) % 2**32 - 2**31
LOW31 = 2147483647
ROW = 1000003
FEAT = 7919
AXES = ("grp", "wide")
LANES = 128
KT = 256
SLAB = 128
SLABS = 12
EARLY = 2
SEQ_BLOCK = 16
PROJECT_VMEM = 36 << 20
FINISH_VMEM = 8 << 20
HALVES = 1


def shift_down(bits, places):
    return lax.shift_right_logical(bits, jnp.int32(places))


def mixed(hashed, wraps):
    top = shift_down(hashed, 16)
    if wraps:
        top = top & 32767
    hashed = (hashed ^ top) * MUL
    return (hashed ^ (shift_down(hashed, 16) & 32767)) * jnp.int32(TOP)


def sign_weights(top):
    return jnp.where(top < 0, -2.0, 0.0).astype(jnp.bfloat16)


def grad_kernel(
    lens_ref,
    seeds_ref,
    grp_ref,
    up_any,
    outg_any,
    hid_any,
    out_ref,
    held_any,
    up_ref,
    outg_ref,
    hid_ref,
    pos_ref,
    turn_ref,
    held_ref,
    sems,
    held_sems,
    *,
    single,
):
    seq = pl.program_id(0)
    blocks, toks, outs = outg_ref.shape
    width = hid_ref.shape[2]
    groups, wide, _, rows, cols = out_ref.shape
    chunk = held_ref.shape[2]
    first_row = grp_ref[0] * rows

    def loads(blk):
        return (
            pltpu.make_async_copy(up_any.at[:, pl.ds(blk * outs, outs)], up_ref.at[blk], sems.at[0, blk]),
            pltpu.make_async_copy(outg_any.at[seq, :, pl.ds(blk * outs, outs)], outg_ref.at[blk], sems.at[1, blk]),
            pltpu.make_async_copy(hid_any.at[seq, :, pl.ds(blk * width, width)], hid_ref.at[blk], sems.at[2, blk]),
        )

    copies = [loads(blk) for blk in range(blocks)]
    for load_up, load_outg, _ in copies:
        load_up.start()
        load_outg.start()
    for _, _, load_hid in copies:
        load_hid.start()

    pieces = held_ref.shape[1] // blocks

    def held_copy(slab, blk):
        span = pl.ds(blk * pieces, pieces)
        return pltpu.make_async_copy(held_ref.at[slab, span], held_any.at[slab, span], held_sems.at[slab, blk])

    def hold(slab, blk):
        def fill():
            span = range(blk * pieces, (blk + 1) * pieces)
            for pair, word in slab_pairs(pos_ref, seeds_ref, turn_ref, first_row, slab, rows, cols // chunk, chunk, span):
                held_ref[slab, pair] = word
            held_copy(slab, blk).start()

        once(fill)

    def once(task):
        if single:
            task()
        else:
            pl.when(seq == 0)(task)

    def start_hold():
        fill_positions(pos_ref)
        fill_turns(turn_ref, seeds_ref, first_row, rows)

    once(start_hold)
    for slab in range(EARLY):
        for blk in range(blocks):
            hold(slab, blk)
    low = jnp.zeros((toks, up_ref.shape[1]), jnp.float32)
    for blk, (load_up, load_outg, _) in enumerate(copies):
        load_up.wait()
        load_outg.wait()
        low += lax.dot_general(
            outg_ref[blk], up_ref[blk], (((1,), (1,)), ((), ())), preferred_element_type=jnp.float32
        )
    live = lax.broadcasted_iota(jnp.int32, low.shape, 0) < lens_ref[seq]
    low = jnp.where(live, low, 0.0).T.astype(jnp.bfloat16)
    count = lens_ref[seq].astype(jnp.float32)
    for blk, (_, _, load_hid) in enumerate(copies):
        load_hid.wait()
        summed = jnp.dot(low, hid_ref[blk], preferred_element_type=jnp.float32)
        grad = (summed / count).astype(jnp.bfloat16)
        for grp in range(groups):
            for own in range(width // cols):
                out_ref[grp, blk * (width // cols) + own, 0] = grad[
                    grp * rows : (grp + 1) * rows, own * cols : (own + 1) * cols
                ]

    def end_hold():
        for slab in range(EARLY):
            for blk in range(blocks):
                held_copy(slab, blk).wait()

    once(end_hold)


def seq_grads(hidden, output_gradient, adapter_up_factor, lengths, seeds, grp, groups, wide):
    seqs, toks, width = hidden.shape
    outs, rank = adapter_up_factor.shape
    rows, cols = rank // groups, width // wide
    chunk = min(256, cols)
    pairs = rows * cols // chunk // 2
    blocks = 4
    return pl.pallas_call(
        functools.partial(grad_kernel, single=seqs == 1),
        out_shape=(
            jax.ShapeDtypeStruct((groups, wide, seqs, rows, cols), jnp.bfloat16),
            jax.ShapeDtypeStruct((SLABS, pairs, chunk, SLAB), jnp.int32),
        ),
        grid_spec=pltpu.PrefetchScalarGridSpec(
            num_scalar_prefetch=3,
            grid=(seqs,),
            in_specs=[pl.BlockSpec(memory_space=pl.ANY)] * 3,
            out_specs=(
                pl.BlockSpec((groups, wide, 1, rows, cols), lambda s, *_: (0, 0, s, 0, 0)),
                pl.BlockSpec(memory_space=pl.ANY),
            ),
            scratch_shapes=[
                pltpu.VMEM((blocks, rank, outs // blocks), jnp.bfloat16),
                pltpu.VMEM((blocks, toks, outs // blocks), jnp.bfloat16),
                pltpu.VMEM((blocks, toks, width // blocks), jnp.bfloat16),
                pltpu.VMEM((CB, SLAB), jnp.int32),
                pltpu.SMEM((cols // CB,), jnp.int32),
                pltpu.VMEM((EARLY, pairs, chunk, SLAB), jnp.int32),
                pltpu.SemaphoreType.DMA((3, blocks)),
                pltpu.SemaphoreType.DMA((EARLY, blocks)),
            ],
        ),
        name="seq_grads",
    )(lengths, seeds, grp, adapter_up_factor.T, output_gradient, hidden)


def fill_positions(pos_ref):
    pos_ref[...] = (
        lax.broadcasted_iota(jnp.int32, pos_ref.shape, 0) * ROW
        + lax.broadcasted_iota(jnp.int32, pos_ref.shape, 1) * FEAT
    )


BLOCK = CB * ROW
SPAN = (CB - 1) * ROW + (K - 1) * FEAT
EDGE = 2**31 - SPAN


def fill_turns(turn_ref, seeds_ref, first_row, rows):
    for pos in range(turn_ref.shape[0]):
        short = EDGE - ((seeds_ref[pos] + first_row * BLOCK) & LOW31)
        turn_ref[pos] = lax.div(jnp.maximum(short + (BLOCK - 1), 0), jnp.int32(BLOCK)) + 2


def slot_row(turn, slot, rows):
    if rows & (rows - 1) == 0:
        return (turn + slot) & (rows - 1)
    return lax.rem(turn + slot, jnp.int32(rows))


def slot_wraps(slot, rows):
    return slot >= rows - 2 or rows * BLOCK + SPAN > 2**31


def slab_pairs(pos_ref, seeds_ref, turn_ref, first_row, slab, rows, halves, chunk, pairs):
    def top_of(entry):
        slot, half = divmod(entry, halves)
        return slot_tile(pos_ref, seeds_ref, turn_ref, first_row, slab * SLAB, slot, half, chunk // CB, rows)

    for pair in pairs:
        yield pair, top_of(2 * pair) | shift_down(top_of(2 * pair + 1), 17)


def slot_tile(pos_ref, seeds_ref, turn_ref, first_row, feat, slot, half, parts, rows):
    tile = []
    for part in range(half * parts, (half + 1) * parts):
        row = first_row + slot_row(turn_ref[part], slot, rows)
        tile.append(pos_ref[...] + ((seeds_ref[part] + row * BLOCK + feat * FEAT) & LOW31))
    return mixed(jnp.concatenate(tile, axis=0) if parts > 1 else tile[0], slot_wraps(slot, rows))


def presign_kernel(seeds_ref, grp_ref, early_ref, out_ref, pos_ref, turn_ref, *, rows, halves):
    slab, side = pl.program_id(0), pl.program_id(1)
    first_row = grp_ref[0] * rows
    pairs, chunk = out_ref.shape[1:3]

    @pl.when((slab == 0) & (side == 0))
    def _():
        fill_positions(pos_ref)
        fill_turns(turn_ref, seeds_ref, first_row, rows)

    def fill(first):
        span = range(first, first + pairs)
        for pair, word in slab_pairs(pos_ref, seeds_ref, turn_ref, first_row, EARLY + slab, rows, halves, chunk, span):
            out_ref[0, pair - first] = word

    for pos in range(HALVES):
        pl.when(side == pos)(functools.partial(fill, pos * pairs))


def presign(seeds, grp, held, rows, cols):
    chunk = min(256, cols)
    chunks = rows * cols // chunk
    return pl.pallas_call(
        functools.partial(presign_kernel, rows=rows, halves=cols // chunk),
        out_shape=jax.ShapeDtypeStruct((SLABS, chunks // 2, chunk, SLAB), jnp.int32),
        grid_spec=pltpu.PrefetchScalarGridSpec(
            num_scalar_prefetch=2,
            grid=(SLABS - EARLY, HALVES),
            in_specs=[pl.BlockSpec(memory_space=pl.ANY)],
            out_specs=pl.BlockSpec((1, chunks // 2 // HALVES, chunk, SLAB), lambda i, j, s, g: (EARLY + i, j, 0, 0)),
            scratch_shapes=[pltpu.VMEM((CB, SLAB), jnp.int32), pltpu.SMEM((cols // CB,), jnp.int32)],
        ),
        cost_estimate=pl.CostEstimate(
            flops=SLABS * SLAB * rows * cols * 10, bytes_accessed=SLABS * SLAB * rows * cols * 2, transcendentals=0
        ),
        input_output_aliases={2: 0},
        name="presign",
    )(seeds, grp, held)


def project_kernel(
    seeds_ref,
    grp_ref,
    grad_ref,
    first_ref,
    second_ref,
    held_any,
    out_ref,
    feat_ref,
    wide_ref,
    upd_ref,
    sum_ref,
    pos_ref,
    turn_ref,
    held_ref,
    held_sems,
):
    step = pl.program_id(0)
    steps = pl.num_programs(0)
    twice = SLABS - steps
    seqs, rows, cols = grad_ref.shape
    chunk = upd_ref.shape[2]
    halves = cols // chunk
    parts = chunk // CB
    first_row = grp_ref[0] * rows

    def held_copy(slab, spot):
        return pltpu.make_async_copy(held_any.at[slab], held_ref.at[spot], held_sems.at[spot])

    @pl.when(step == 0)
    def _():
        for spot in range(2):
            held_copy(spot, spot).start()
        for pos in range(twice):
            held_copy(steps + pos, 2 + pos).start()
        fill_positions(pos_ref)
        fill_turns(turn_ref, seeds_ref, first_row, rows)
        width = min(LANES, cols)

        def update_step(blk, carry):
            at = pl.ds(pl.multiple_of(blk * SEQ_BLOCK, SEQ_BLOCK), SEQ_BLOCK)
            for row in range(0, rows, 8):
                for lane in range(0, cols, LANES):
                    spot = (slice(row, row + 8), slice(lane, lane + width))
                    grad = grad_ref[(at, *spot)].astype(jnp.float32)
                    first_new = 0.9 * first_ref[spot] + 0.1 * grad
                    second_new = 0.999 * second_ref[spot] + 0.001 * grad * grad
                    update = first_new / (jnp.sqrt(second_new) + 1e-08)
                    update = jnp.swapaxes(update, 0, 1).astype(jnp.bfloat16)
                    wide_ref[lane // LANES, row : row + 8, at, :width] = update
            return carry

        lax.fori_loop(0, seqs // SEQ_BLOCK, update_step, 0)
        total = jnp.zeros((seqs, width), jnp.float32)
        lanes = lax.broadcasted_iota(jnp.int32, (seqs, LANES), 1)
        for entry in range(upd_ref.shape[0]):
            slot, half = divmod(entry, halves)
            for lane in range(0, chunk, LANES):
                spot = half * chunk + lane
                upd = wide_ref[spot // LANES, slot_row(turn_ref[spot // CB], slot, rows)]
                for pos in range(CB, width, CB):
                    row = slot_row(turn_ref[(spot + pos) // CB], slot, rows)
                    upd = jnp.where(lanes < pos, upd, wide_ref[spot // LANES, row])
                upd = upd[:, :width]
                upd_ref[entry, :, lane : lane + width] = upd
                total += upd.astype(jnp.float32)
        sum_ref[...] = jnp.broadcast_to(jnp.sum(total, axis=1, keepdims=True), sum_ref.shape)

    feats = feat_ref.shape[0] // seqs
    held_feats = SLABS * SLAB
    start = jnp.broadcast_to(sum_ref[:, :1], (seqs, KT))

    def put(first_feat, acc):
        for part in range(acc.shape[1] // LANES):
            feat_ref[pl.ds(first_feat // LANES + part, seqs, stride=feats), :] = acc[:, part * LANES : (part + 1) * LANES]

    def tile_step(slabs):
        feat = held_feats + step * KT
        accs = [start] + [start[:, :SLAB]] * len(slabs)
        for slab, spot in slabs:
            held_copy(slab, spot).wait()
        for entry in range(upd_ref.shape[0]):
            slot, half = divmod(entry, halves)
            tops = [slot_tile(pos_ref, seeds_ref, turn_ref, first_row, feat, slot, half, parts, rows)]
            words = [held_ref[spot, entry // 2] for _, spot in slabs]
            tops += [word << 17 if entry % 2 else word for word in words]
            for pos, top in enumerate(tops):
                accs[pos] += jnp.dot(upd_ref[entry], sign_weights(top), preferred_element_type=jnp.float32)
        put(feat, accs[0])
        for (slab, _), acc in zip(slabs, accs[1:]):
            put(slab * SLAB, acc)

    spot = lax.rem(step, 2)
    pl.when(step < steps - twice)(lambda: tile_step([(step, spot)]))
    pl.when(step >= steps - twice)(lambda: tile_step([(step, spot), (step + twice, step - (steps - twice) + 2)]))

    @pl.when(step + 2 < steps)
    def _():
        held_copy(step + 2, spot).start()

    @pl.when(step == steps - 1)
    def _():
        out_ref[...] = feat_ref[...].astype(out_ref.dtype)


def project(grads, first, second, seeds, grp, held):
    seqs, rows, cols = grads.shape
    chunk = min(256, cols)
    chunks = rows * cols // chunk
    feats = K // LANES
    steps = (K - SLABS * SLAB) // KT
    return pl.pallas_call(
        project_kernel,
        out_shape=jax.ShapeDtypeStruct((seqs * feats, LANES), jnp.bfloat16),
        grid_spec=pltpu.PrefetchScalarGridSpec(
            num_scalar_prefetch=2,
            grid=(steps,),
            in_specs=[
                pl.BlockSpec(memory_space=pltpu.VMEM),
                pl.BlockSpec((rows, cols), lambda i, s, g: (g[0], 0)),
                pl.BlockSpec((rows, cols), lambda i, s, g: (g[0], 0)),
                pl.BlockSpec(memory_space=pl.ANY),
            ],
            out_specs=pl.BlockSpec((seqs * feats, LANES), lambda i, s, g: (0, 0)),
            scratch_shapes=[
                pltpu.VMEM((seqs * feats, LANES), jnp.float32),
                pltpu.VMEM((pl.cdiv(cols, LANES), rows, seqs, LANES), jnp.bfloat16),
                pltpu.VMEM((chunks, seqs, chunk), jnp.bfloat16),
                pltpu.VMEM((seqs, LANES), jnp.float32),
                pltpu.VMEM((CB, KT), jnp.int32),
                pltpu.SMEM((cols // CB,), jnp.int32),
                pltpu.VMEM((2 + SLABS - steps, chunks // 2, chunk, SLAB), jnp.int32),
                pltpu.SemaphoreType.DMA((2 + SLABS - steps,)),
            ],
        ),
        compiler_params=pltpu.CompilerParams(vmem_limit_bytes=PROJECT_VMEM),
        name="project",
    )(seeds, grp, grads, first, second, held)


def finish_kernel(partial_ref, out_ref):
    total = jnp.sum(partial_ref[...].astype(jnp.float32), axis=0)
    mean = jnp.sum(total * total, axis=(1, 2), keepdims=True) / K
    out_ref[...] = total * lax.rsqrt(mean + 1e-06)


def shards(
    hidden,
    output_gradient,
    adapter_up_factor,
    first_moment_estimate,
    second_moment_estimate,
    lengths,
    seeds,
):
    groups, wide = lax.axis_size("grp"), lax.axis_size("wide")
    devices = groups * wide
    own_seqs = hidden.shape[0]
    grp = lax.axis_index("grp").astype(jnp.int32).reshape(1)
    grads, held = seq_grads(hidden, output_gradient, adapter_up_factor, lengths, seeds, grp, groups, wide)
    rows, cols = grads.shape[-2:]
    grads = grads.reshape(devices, own_seqs, rows, cols)
    held = presign(seeds, grp, held, rows, cols)
    grads = lax.all_to_all(grads, AXES, 0, 0, tiled=True).reshape(devices * own_seqs, rows, cols)
    grads = pltpu.with_memory_space_constraint(grads, pltpu.VMEM)
    partial = project(grads, first_moment_estimate, second_moment_estimate, seeds, grp, held)
    partial = partial.reshape(devices, own_seqs, K // LANES, LANES)
    partial = lax.all_to_all(partial, AXES, 0, 0, tiled=True)
    partial = pltpu.with_memory_space_constraint(partial, pltpu.VMEM)
    out = pl.pallas_call(
        finish_kernel,
        out_shape=jax.ShapeDtypeStruct((own_seqs, K // LANES, LANES), jnp.float32),
        in_specs=[pl.BlockSpec(memory_space=pltpu.VMEM)],
        compiler_params=pltpu.CompilerParams(vmem_limit_bytes=FINISH_VMEM),
        name="finish",
    )(partial)
    return out.reshape(own_seqs, K)


def solution(mesh):
    placed = (
        P(AXES, None, None),
        P(AXES, None, None),
        P(),
        P(None, "wide"),
        P(None, "wide"),
        P(AXES),
        P("wide"),
    )
    with jax.sharding.use_abstract_mesh(mesh.abstract_mesh):
        return jax.shard_map(shards, mesh=mesh, in_specs=placed, out_specs=P(AXES, None), check_vma=False)
```
